32 devices in a mesh: dp: 2 (over x), context: 4 (over z), tensor: 4 (over y, core).
Axes of the slice: x: 2, y: 2, z: 4, core: 2. Of those that a mesh axis runs over, the one named last changes fastest.
Arguments:
- tokens: bfloat16 [6144, 640], P(('dp', 'context')), may hold values from -8 to 8
- seq_lengths: int32 [2, 2], P('dp'), may hold values from 1 to 2048, 3072 in all within a row
- input_gain: bfloat16 [640], P('dp'), may hold values from 0.25 to 1.75
- query_weight: bfloat16 [640, 1024], P('dp', 'tensor'), may hold values from -0.25 to 0.25
- key_weight: bfloat16 [640, 256], P('dp'), may hold values from -0.25 to 0.25
- value_weight: bfloat16 [640, 256], P('dp'), may hold values from -0.25 to 0.25
- query_gain: bfloat16 [256], P('dp'), may hold values from 0.25 to 1.75
- key_gain: bfloat16 [256], P('dp'), may hold values from 0.25 to 1.75
- output_weight: bfloat16 [1024, 640], P('tensor', 'dp'), may hold values from -0.1875 to 0.1875
- attention_gain: bfloat16 [640], P('dp'), may hold values from 0.25 to 1.75
- prefeed_gain: bfloat16 [640], P('dp'), may hold values from 0.25 to 1.75
- gate_weight: bfloat16 [640, 2048], P('dp', 'tensor'), may hold values from -0.25 to 0.25
- up_weight: bfloat16 [640, 2048], P('dp', 'tensor'), may hold values from -0.25 to 0.25
- down_weight: bfloat16 [2048, 640], P('tensor', 'dp'), may hold values from -0.125 to 0.125
- feed_gain: bfloat16 [640], P('dp'), may hold values from 0.25 to 1.75
- cotangent: bfloat16 [6144, 640], P(('dp', 'context')), may hold values from -8 to 8
Outputs:
- layer_out: bfloat16 [6144, 640], P(('dp', 'context'))
- tokens_grad: float32 [6144, 640], P(('dp', 'context'))
- input_gain_grad: float32 [640], P('dp')
- query_weight_grad: float32 [640, 1024], P('dp', 'tensor')
- key_weight_grad: float32 [640, 256], P('dp')
- value_weight_grad: float32 [640, 256], P('dp')
- query_gain_grad: float32 [256], P('dp')
- key_gain_grad: float32 [256], P('dp')
- output_weight_grad: float32 [1024, 640], P('tensor', 'dp')
- attention_gain_grad: float32 [640], P('dp')
- prefeed_gain_grad: float32 [640], P('dp')
- gate_weight_grad: float32 [640, 2048], P('dp', 'tensor')
- up_weight_grad: float32 [640, 2048], P('dp', 'tensor')
- down_weight_grad: float32 [2048, 640], P('tensor', 'dp')
- feed_gain_grad: float32 [640], P('dp')
The draws below stay inside these ranges and needn't reach their ends.
Inputs may be any that keep to these rules, and one draw needn't show every extreme that they name: `seq_lengths`: each row lists 2 lengths that add up to 3072, none above 2048.
All inputs are finite; a program needn't handle non-finite values.
Results may differ from the reference program's by a relative error of at most 0.022.
Values may be sent and summed in bfloat16 or wider, within the bound.
No kernel may reach another device: no remote copies, remote signals or barrier semaphores. Data moves between devices by JAX's collectives and lax.ppermute only.
A program may use at most 128 MiB of HBM per device.

```python
import math
import jax
import jax.numpy as jnp
import numpy as np
from jax import lax

D = 640
HEADS = 4
HD = 256
FF = 2048
TOK_DEV = 768
GROUP = 3072
MOST = 2048
SEQS = 2
TOKENS = 6144
N_DP = 2


def raised(drawn, key, source, target, shards_of, factor):
    def block_of(dim):
        return (jnp.arange(drawn.shape[dim]) // (drawn.shape[dim] // shards_of)).reshape((-1,) + (1,) * (drawn.ndim - 1 - dim))

    first = jax.random.permutation(key, shards_of)[block_of(target)]
    other_side = (block_of(target) + shards_of // 2) % shards_of
    return jnp.where((block_of(source) == first) | (block_of(source) == other_side), factor * drawn, drawn)


def level_of(stream_key, extent, shards, least, top_value):
    loudness = 1.0
    for dim, blocks in shards:
        heights = jax.random.uniform(jax.random.fold_in(jax.random.fold_in(stream_key, 6), dim), (blocks,), jnp.float32, least / len(shards), top_value / len(shards))
        loudness = loudness * jnp.repeat(jnp.exp(heights), extent[dim] // blocks).reshape((-1,) + (1,) * (len(extent) - 1 - dim))
    return loudness


def profile(count, total, limit, skew):
    portions = [(1 << 20) // math.isqrt(grade ** skew) + 1 for grade in range(2, count + 1)]
    surplus, holding = total - limit - (count - 1), [1] * (count - 1)
    while surplus > 0:
        free = [i for i in range(count - 1) if holding[i] < limit]
        mass, budget = sum([portions[i] for i in free]), surplus
        for i in free:
            addition = min(limit - holding[i], max(1, budget * portions[i] // mass), surplus)
            holding[i] = holding[i] + addition
            surplus = surplus - addition
    return np.array([limit] + holding)


def ragged_sizes(key, count, total, bound, skew):
    if count == 2:
        one = jax.random.randint(key, (), max(1, total - bound), min(bound, total - 1) + 1)
        return jnp.stack([one, total - one])
    sizes = jnp.asarray(profile(count, total, bound, skew), jnp.int32)
    couples = (count - 1) // 2
    donor, taker = sizes[1:1 + 2 * couples:2], sizes[2:2 + 2 * couples:2]
    room = jnp.minimum(donor - 1, bound - taker)
    passed = jax.random.randint(jax.random.fold_in(key, 1), (couples,), 0, 1 << 20) % (room + 1)
    sizes = sizes.at[1:1 + 2 * couples:2].set(donor - passed).at[2:2 + 2 * couples:2].set(taker + passed)
    return sizes[jax.random.permutation(jax.random.fold_in(key, 2), count)]


def normal_values(key, extent, width, bound, cuts=(), kind=jnp.bfloat16):
    array = width * jax.random.normal(key, extent, jnp.float32)
    if cuts:
        array = array * level_of(key, extent, cuts, -0.22, 0.18)
    return jnp.clip(array, -bound, bound).astype(kind)


def gaussian_with(own_key, shape, scale, limit, split, heavy, held_as=jnp.bfloat16):
    entries = scale * jax.random.normal(own_key, shape, jnp.float32)
    if split:
        entries = entries * level_of(own_key, shape, split, -0.22, 0.18)
    return jnp.clip(raised(entries, jax.random.fold_in(own_key, 3), *heavy), -limit, limit).astype(held_as)


def setup_inputs(seed: int = 0) -> dict:
    keys = jax.random.split(jax.random.key(seed), 17)
    return {
        "tokens": gaussian_with(keys[0], (TOKENS, D), 1.0, 8.0, ((0, 8),), (0, 1, 8, 2.0)),
        "seq_lengths": jax.vmap(lambda own: ragged_sizes(own, SEQS, GROUP, MOST, 2))(jax.random.split(keys[1], N_DP)).reshape((N_DP, SEQS)).astype(jnp.int32),
        "input_gain": jnp.clip(1.0 + 0.15 * jax.random.normal(keys[2], (D,), jnp.float32), 0.25, 1.75).astype(jnp.bfloat16),
        "query_weight": normal_values(keys[3], (D, HEADS * HD), D ** -0.5, 0.25, ((0, 2), (1, 4))),
        "key_weight": normal_values(keys[4], (D, HD), D ** -0.5, 0.25, ((0, 2),)),
        "value_weight": normal_values(keys[5], (D, HD), D ** -0.5, 0.25, ((0, 2),)),
        "query_gain": jnp.clip(1.0 + 0.15 * jax.random.normal(keys[6], (HD,), jnp.float32), 0.25, 1.75).astype(jnp.bfloat16),
        "key_gain": jnp.clip(1.0 + 0.15 * jax.random.normal(keys[7], (HD,), jnp.float32), 0.25, 1.75).astype(jnp.bfloat16),
        "output_weight": normal_values(keys[8], (HEADS * HD, D), (HEADS * HD) ** -0.5, 0.1875, ((0, 4), (1, 2))),
        "attention_gain": jnp.clip(1.0 + 0.15 * jax.random.normal(keys[9], (D,), jnp.float32), 0.25, 1.75).astype(jnp.bfloat16),
        "prefeed_gain": jnp.clip(1.0 + 0.15 * jax.random.normal(keys[10], (D,), jnp.float32), 0.25, 1.75).astype(jnp.bfloat16),
        "gate_weight": normal_values(keys[11], (D, FF), D ** -0.5, 0.25, ((0, 2), (1, 4))),
        "up_weight": normal_values(keys[12], (D, FF), D ** -0.5, 0.25, ((0, 2), (1, 4))),
        "down_weight": normal_values(keys[13], (FF, D), FF ** -0.5, 0.125, ((0, 4), (1, 2))),
        "feed_gain": jnp.clip(1.0 + 0.15 * jax.random.normal(keys[14], (D,), jnp.float32), 0.25, 1.75).astype(jnp.bfloat16),
        "cotangent": gaussian_with(keys[15], (TOKENS, D), 1.0, 8.0, ((0, 8),), (0, 1, 8, 2.0)),
    }


@jax.custom_vjp
def low(v):
    return lax.optimization_barrier(v.astype(jnp.bfloat16)).astype(jnp.float32)

@jax.custom_vjp
def low_back(v):
    return v

def low_keep(v):
    return (low(v), None)

def low_pass(kept, grad):
    return (grad,)

def back_keep(v):
    return (v, None)

def back_low(kept, grad):
    return (low(grad),)
low.defvjp(low_keep, low_pass)
low_back.defvjp(back_keep, back_low)
EPS = 1e-06
NEG = -1000000000.0
SCALE = 0.0625
HIGH = lax.Precision.HIGHEST

def product(left_side, right_side):
    return jnp.dot(left_side, right_side, precision=HIGH, preferred_element_type=jnp.float32)

def rms_norm(values, scale_gain):
    return values * lax.rsqrt(lax.optimization_barrier(jnp.mean(values * values, axis=-1, keepdims=True)) + EPS) * scale_gain

def rotate(values, position):
    half_width = values.shape[-1] // 2
    frequency = jnp.exp(jnp.arange(half_width, dtype=jnp.float32) * (-2.0 * math.log(1000000.0) / values.shape[-1]))
    angles = position.astype(jnp.float32).reshape((-1,) + (1,) * (values.ndim - 1)) * frequency
    cosines = jnp.cos(angles)
    sines = jnp.sin(angles)
    first_half = values[..., :half_width]
    second_half = values[..., half_width:]
    return jnp.concatenate([first_half * cosines - second_half * sines, second_half * cosines + first_half * sines], axis=-1)

def layout(lengths, row_index):
    seq_ends = jnp.cumsum(lengths).astype(jnp.int32)
    starts = (seq_ends - lengths).astype(jnp.int32)
    member = ((row_index[:, None] >= starts[None, :]) & (row_index[:, None] < seq_ends[None, :])).astype(jnp.int32)
    number = jnp.arange(lengths.shape[0], dtype=jnp.int32)
    segment = (lax.optimization_barrier(jnp.sum(member * (number[None, :] + 1), axis=1)) - 1).astype(jnp.int32)
    position = (row_index - lax.optimization_barrier(jnp.sum(member * starts[None, :], axis=1))).astype(jnp.int32)
    return (segment, position)

def attend(query, key_rot, value, segment):
    block_count = GROUP // TOK_DEV
    query_blocks = query.reshape(N_DP * block_count, TOK_DEV, HEADS, HD)
    group_keys = key_rot.reshape(N_DP, GROUP, HD)
    group_values = value.reshape(N_DP, GROUP, HD)
    group_segments = segment.reshape(N_DP, GROUP)
    numbers = jnp.arange(N_DP * block_count, dtype=jnp.int32)

    def one_block(item):
        query_block, number = item
        group_index = (number // block_count).astype(jnp.int32)
        first_row = (number % block_count * TOK_DEV).astype(jnp.int32)
        these_keys = group_keys[group_index]
        these_values = group_values[group_index]
        these_segments = group_segments[group_index]
        row_segments = lax.dynamic_slice_in_dim(these_segments, first_row, TOK_DEV)
        query_rows = first_row + jnp.arange(TOK_DEV, dtype=jnp.int32)
        key_rows = jnp.arange(GROUP, dtype=jnp.int32)
        allowed = (row_segments[:, None] == these_segments[None, :]) & (key_rows[None, :] <= query_rows[:, None])
        scores = low_back(jnp.einsum('qhd,kd->hqk', query_block, these_keys, precision=HIGH) * SCALE)
        scores = jnp.where(allowed[None], scores, NEG)
        running_max = lax.optimization_barrier(jnp.max(scores, axis=-1, keepdims=True))
        exponent = jnp.exp(scores - running_max)
        attn_probs = low(exponent / lax.optimization_barrier(jnp.sum(exponent, axis=-1, keepdims=True)))
        return jnp.einsum('hqk,kd->qhd', attn_probs, these_values, precision=HIGH)
    outputs = lax.map(jax.checkpoint(one_block), (query_blocks, numbers))
    return outputs.reshape(TOKENS, HEADS, HD)

def layer(stream, input_gain, query_weight, key_weight, value_weight, query_gain, key_gain, output_weight, attention_gain, prefeed_gain, gate_weight, up_weight, down_weight, feed_gain, segment, position):
    normed = low(rms_norm(stream, input_gain))
    query_raw = low_back(product(normed, query_weight))
    key_raw = low_back(product(normed, key_weight))
    value = low(low_back(product(normed, value_weight)))
    query = low(rotate(rms_norm(query_raw.reshape(TOKENS, HEADS, HD), query_gain), position))
    key_rot = low(rotate(rms_norm(key_raw, key_gain), position))
    heads_out = low(low_back(attend(query, key_rot, value, segment)))
    attn_sum = low_back(product(heads_out.reshape(TOKENS, HEADS * HD), output_weight))
    middle = stream + rms_norm(attn_sum, attention_gain)
    normed_feed = low(rms_norm(middle, prefeed_gain))
    gate_proj = low_back(product(normed_feed, gate_weight))
    up_proj = low_back(product(normed_feed, up_weight))
    hidden = low(jax.nn.gelu(gate_proj, approximate=True) * up_proj)
    feed_sum = low_back(product(hidden, down_weight))
    return middle + rms_norm(feed_sum, feed_gain)

def reference(tokens, seq_lengths, input_gain, query_weight, key_weight, value_weight, query_gain, key_gain, output_weight, attention_gain, prefeed_gain, gate_weight, up_weight, down_weight, feed_gain, cotangent):
    row_index = jnp.arange(GROUP, dtype=jnp.int32)
    segment, position = jax.vmap(lambda lengths: layout(lengths, row_index))(seq_lengths)
    segment = segment.reshape(TOKENS)
    position = position.reshape(TOKENS)

    def forward(stream, *params):
        return layer(stream, *params, segment, position)
    params = (input_gain, query_weight, key_weight, value_weight, query_gain, key_gain, output_weight, attention_gain, prefeed_gain, gate_weight, up_weight, down_weight, feed_gain)
    params = tuple((weight.astype(jnp.float32) for weight in params))
    result, pullback = jax.vjp(forward, tokens.astype(jnp.float32), *params)
    grads = pullback(cotangent.astype(jnp.float32))
    return (result.astype(jnp.bfloat16), grads[0], grads[1], grads[2], grads[3], grads[4], grads[5], grads[6], grads[7], grads[8], grads[9], grads[10], grads[11], grads[12], grads[13])
```

```python
import math

import jax
import jax.numpy as jnp
from jax import lax
from jax.sharding import PartitionSpec as P

HD = 256
LMAX = 2048
EPS = 1e-06
SCALE = 0.0625

BF = jnp.bfloat16
F32 = jnp.float32


def product(left_side, right_side):
    return jnp.dot(left_side, right_side, preferred_element_type=F32)


def product_lt(left_side, right_side):
    return lax.dot_general(
        left_side, right_side, (((0,), (0,)), ((), ())), preferred_element_type=F32
    )


def product_rt(left_side, right_side):
    return lax.dot_general(
        left_side, right_side, (((1,), (1,)), ((), ())), preferred_element_type=F32
    )


def low(values):
    return lax.reduce_precision(values, 8, 7).astype(BF)


def over_core(array):
    devices = lax.axis_size("tensor")
    return lax.ppermute(array, "tensor", [(i, i ^ 1) for i in range(devices)])


def over_pairs(array):
    devices = lax.axis_size("tensor")
    return lax.ppermute(array, "tensor", [(i, i ^ 2) for i in range(devices)])


def over_context(array, by):
    devices = lax.axis_size("context")
    pairs = [(i, i + by) for i in range(devices) if 0 <= i + by < devices]
    return lax.ppermute(array, "context", pairs)


def after(array, earlier):
    return lax.optimization_barrier((array, earlier))[0]


def ordered(place, mine, other):
    return jnp.where(
        place == 0,
        jnp.concatenate([mine, other], axis=0),
        jnp.concatenate([other, mine], axis=0),
    )


def pairs_sum(partial):
    short = low(partial)
    return short.astype(F32) + over_pairs(short).astype(F32)


def dp_gathered(array):
    if lax.axis_size("dp") == 2:
        other = lax.ppermute(array, "dp", [(0, 1), (1, 0)])
        return ordered(lax.axis_index("dp"), array, other)
    return lax.all_gather(array, "dp", axis=0, tiled=True)


def dp_scattered(total):
    if lax.axis_size("dp") == 2:
        place = lax.axis_index("dp")
        rows = total.shape[0] // 2
        keep = lax.dynamic_slice_in_dim(total, place * rows, rows, 0)
        send = lax.dynamic_slice_in_dim(total, (1 - place) * rows, rows, 0)
        return keep.astype(F32) + lax.ppermute(low(send), "dp", [(0, 1), (1, 0)]).astype(F32)
    return lax.psum_scatter(low(total), "dp", scatter_dimension=0, tiled=True).astype(F32)


def context_sum(total):
    if lax.axis_size("context") != 4:
        return lax.psum(total, "context")
    place = lax.axis_index("context")
    near, far = place % 2, place // 2
    rows = total.shape[0] // 2
    keep = lax.dynamic_slice_in_dim(total, near * rows, rows, 0)
    send = lax.dynamic_slice_in_dim(total, (1 - near) * rows, rows, 0)
    by_near = [(i, i ^ 1) for i in range(4)]
    by_far = [(i, i ^ 2) for i in range(4)]
    part = keep + lax.ppermute(low(send), "context", by_near).astype(F32)
    rows = rows // 2
    keep = lax.dynamic_slice_in_dim(part, far * rows, rows, 0)
    send = lax.dynamic_slice_in_dim(part, (1 - far) * rows, rows, 0)
    part = low(keep + lax.ppermute(low(send), "context", by_far).astype(F32))
    part = ordered(far, part, lax.ppermute(part, "context", by_far))
    return ordered(near, part, lax.ppermute(part, "context", by_near)).astype(F32)


def context_sum_small(total):
    if lax.axis_size("context") != 4:
        return lax.psum(total, "context")
    for bit in (1, 2):
        short = low(total)
        other = lax.ppermute(short, "context", [(i, i ^ bit) for i in range(4)])
        total = short.astype(F32) + other.astype(F32)
    return total


def normed_of(values):
    inverse = lax.rsqrt(jnp.mean(values * values, axis=-1, keepdims=True) + EPS)
    return values * inverse, inverse


def norm_back(grad, gain, unit, inverse):
    scaled = grad * gain
    return inverse * (scaled - unit * jnp.mean(scaled * unit, axis=-1, keepdims=True))


def turned(values, cosines, sines):
    half_width = values.shape[-1] // 2
    first_half = values[..., :half_width]
    second_half = values[..., half_width:]
    return jnp.concatenate(
        [first_half * cosines - second_half * sines, second_half * cosines + first_half * sines],
        axis=-1,
    )


def local(
    tokens,
    seq_lengths,
    input_gain,
    query_weight,
    key_weight,
    value_weight,
    query_gain,
    key_gain,
    output_weight,
    attention_gain,
    prefeed_gain,
    gate_weight,
    up_weight,
    down_weight,
    feed_gain,
    cotangent,
):
    block_rows = tokens.shape[0]
    rows = block_rows // 2
    width = tokens.shape[1]
    context_place = lax.axis_index("context")
    core = lax.axis_index("tensor") % 2
    pair = lax.axis_index("tensor") // 2
    reach = min(lax.axis_size("context") - 1, (LMAX - 2) // block_rows + 1)
    dp_count = lax.axis_size("dp")
    shard = width // dp_count
    feed_width = gate_weight.shape[1]

    gains = jnp.concatenate(
        [input_gain, attention_gain, prefeed_gain, feed_gain, query_gain, key_gain]
    ).reshape(1, -1)
    gain_parts = lax.all_gather(gains, "dp", axis=0, tiled=True)
    kv_pack = jnp.concatenate([key_weight, value_weight], axis=1)
    qo_pack = jnp.concatenate([query_weight, output_weight.T], axis=1)
    feed_pack = jnp.concatenate([gate_weight, up_weight, down_weight.T], axis=1)
    w_kv = dp_gathered(kv_pack)
    w_qo = dp_gathered(after(qo_pack, w_kv))
    w_feed = dp_gathered(after(feed_pack, w_qo))
    w_qo_other = over_core(w_qo)
    w_feed_other = over_core(w_feed)

    def gain_of(first, count):
        return gain_parts[:, first : first + count].reshape(1, -1).astype(F32)

    g_input, g_attention, g_prefeed, g_feed = (gain_of(i * shard, shard) for i in range(4))
    head_shard = HD // dp_count
    g_query, g_key = (gain_of(4 * shard + i * head_shard, head_shard) for i in range(2))

    stream = lax.dynamic_slice_in_dim(tokens, core * rows, rows, 0).astype(F32)
    grad_out = lax.dynamic_slice_in_dim(cotangent, core * rows, rows, 0).astype(F32)
    row_index = (
        context_place * block_rows + core * rows + lax.broadcasted_iota(jnp.int32, (rows, 1), 0)
    )
    start = jnp.zeros_like(row_index)
    begin = jnp.int32(0)
    for number in range(seq_lengths.shape[1]):
        start = jnp.where(row_index >= begin, begin, start)
        begin = begin + seq_lengths[0, number]
    frequency = jnp.exp(
        lax.broadcasted_iota(jnp.int32, (1, HD // 2), 1).astype(F32)
        * (-2.0 * math.log(1000000.0) / HD)
    )
    angles = (row_index - start).astype(F32) * frequency
    cosines, sines = lax.optimization_barrier((jnp.cos(angles), jnp.sin(angles)))
    two_cosines = jnp.concatenate([cosines, cosines], axis=0)
    two_sines = jnp.concatenate([sines, sines], axis=0)

    input_unit, input_inverse = normed_of(stream)
    normed = (input_unit * g_input).astype(BF)

    key_value_raw = product(normed, w_kv)
    key_unit, key_inverse = normed_of(key_value_raw[:, :HD])
    key_own = turned(key_unit * g_key, cosines, sines).astype(BF)
    value_own = key_value_raw[:, HD:].astype(BF)
    blocks = []
    current = (key_own, value_own)
    for step in range(reach + 1):
        if step > 0:
            current = (over_context(current[0], 1), over_context(current[1], 1))
        blocks.append(
            (
                jnp.concatenate([current[0], over_core(current[0])], axis=0),
                jnp.concatenate([current[1], over_core(current[1])], axis=0),
            )
        )

    query_raw = jnp.concatenate(
        [product(normed, w_qo[:, :HD]), product(normed, w_qo_other[:, :HD])], axis=0
    )
    query_unit, query_inverse = normed_of(query_raw)
    query = turned(query_unit * g_query, two_cosines, two_sines).astype(BF)

    two_rows = jnp.concatenate([row_index, row_index], axis=0)
    two_starts = jnp.concatenate([start, start], axis=0)
    within = lax.broadcasted_iota(jnp.int32, (1, rows), 1)
    key_rows = jnp.concatenate([core * rows + within, (1 - core) * rows + within], axis=1)
    kept = []
    mass = jnp.zeros((2 * rows, 1), F32)
    heads_sum = jnp.zeros((2 * rows, HD), F32)
    for step in range(reach + 1):
        key_block, value_block = blocks[step]
        key_index = (context_place - step) * block_rows + key_rows
        allowed = (key_index >= two_starts) & (key_index <= two_rows)
        weights = jnp.where(allowed, jnp.exp(product_rt(query, key_block) * SCALE), 0.0)
        mass = mass + jnp.sum(weights, axis=1, keepdims=True)
        weights = weights.astype(BF)
        heads_sum = heads_sum + product(weights, value_block)
        kept.append(weights)
    inverse_mass = 1.0 / mass
    heads = heads_sum * inverse_mass
    heads_low = heads.astype(BF)
    heads_wide = jnp.concatenate([heads_low[:rows], heads_low[rows:]], axis=1)
    w_output = jnp.concatenate([w_qo[:, HD:], w_qo_other[:, HD:]], axis=1)
    attn_sum = pairs_sum(product_rt(heads_wide, w_output))

    w_gate_up = jnp.concatenate(
        [
            w_feed[:, :feed_width],
            w_feed_other[:, :feed_width],
            w_feed[:, feed_width : 2 * feed_width],
            w_feed_other[:, feed_width : 2 * feed_width],
        ],
        axis=1,
    )
    w_down = jnp.concatenate([w_feed[:, 2 * feed_width :], w_feed_other[:, 2 * feed_width :]], axis=1)
    attn_unit, attn_inverse = normed_of(attn_sum)
    middle = stream + attn_unit * g_attention
    middle_unit, middle_inverse = normed_of(middle)
    normed_feed = (middle_unit * g_prefeed).astype(BF)
    gate_up = product(normed_feed, w_gate_up)
    activation, activation_back = jax.vjp(
        lambda gate_part, up_part: jax.nn.gelu(gate_part, approximate=True) * up_part,
        gate_up[:, : 2 * feed_width],
        gate_up[:, 2 * feed_width :],
    )
    hidden = activation.astype(BF)
    feed_sum = pairs_sum(product_rt(hidden, w_down))
    feed_unit, feed_inverse = normed_of(feed_sum)
    layer_own = low(middle + feed_unit * g_feed)
    layer_out = ordered(core, layer_own, over_core(layer_own))

    grad_gfeed = jnp.sum(grad_out * feed_unit, axis=0, keepdims=True)
    grad_feed = norm_back(grad_out, g_feed, feed_unit, feed_inverse).astype(BF)
    grad_gate_full, grad_up_full = activation_back(product(grad_feed, w_down))
    grad_gate_up = jnp.concatenate([grad_gate_full.astype(BF), grad_up_full.astype(BF)], axis=1)
    grad_normed_feed = pairs_sum(product_rt(grad_gate_up, w_gate_up))

    def shared(total, own, other):
        mine = jnp.concatenate([total[:, a:b] for a, b in own], axis=1)
        theirs = jnp.concatenate([total[:, a:b] for a, b in other], axis=1)
        whole = mine + over_core(low(theirs)).astype(F32)
        return context_sum(dp_scattered(whole))

    total_down = shared(
        product_lt(grad_feed, hidden), [(0, feed_width)], [(feed_width, 2 * feed_width)]
    )
    total_gate_up = shared(
        product_lt(normed_feed, grad_gate_up),
        [(0, feed_width), (2 * feed_width, 3 * feed_width)],
        [(feed_width, 2 * feed_width), (3 * feed_width, 4 * feed_width)],
    )

    grad_gprefeed = jnp.sum(grad_normed_feed * middle_unit, axis=0, keepdims=True)
    grad_middle = grad_out + norm_back(grad_normed_feed, g_prefeed, middle_unit, middle_inverse)
    grad_gattention = jnp.sum(grad_middle * attn_unit, axis=0, keepdims=True)
    grad_attn = norm_back(grad_middle, g_attention, attn_unit, attn_inverse).astype(BF)

    grad_heads_wide = product(grad_attn, w_output)
    grad_heads = jnp.concatenate([grad_heads_wide[:, :HD], grad_heads_wide[:, HD:]], axis=0)
    grad_heads_low = (grad_heads * inverse_mass).astype(BF)
    row_dots = jnp.sum(grad_heads * heads, axis=1, keepdims=True) * inverse_mass
    grad_query = jnp.zeros((2 * rows, HD), F32)
    carried = None
    for step in range(reach, -1, -1):
        key_block, value_block = blocks[step]
        weights = kept[step]
        grad_scores = (
            weights.astype(F32) * (product_rt(grad_heads_low, value_block) - row_dots)
        ).astype(BF)
        grad_query = grad_query + product(grad_scores, key_block)
        value_part = product_lt(weights, grad_heads_low)
        key_part = product_lt(grad_scores, query) * SCALE
        value_sum = value_part[:rows] + over_core(low(value_part[rows:])).astype(F32)
        key_sum = key_part[:rows] + over_core(low(key_part[rows:])).astype(F32)
        if carried is not None:
            value_sum = value_sum + carried[0].astype(F32)
            key_sum = key_sum + carried[1].astype(F32)
        if step > 0:
            carried = (over_context(low(value_sum), -1), over_context(low(key_sum), -1))

    grad_query_turned = turned(grad_query * SCALE, two_cosines, -two_sines)
    grad_gquery = jnp.sum(grad_query_turned * query_unit, axis=0, keepdims=True)
    grad_query_raw = norm_back(grad_query_turned, g_query, query_unit, query_inverse).astype(BF)
    grad_query_wide = jnp.concatenate([grad_query_raw[:rows], grad_query_raw[rows:]], axis=1)
    grad_q_total = product_lt(normed, grad_query_wide)
    grad_o_total = product_lt(grad_attn, heads_wide)
    total_qo = shared(
        jnp.concatenate([grad_q_total, grad_o_total], axis=1),
        [(0, HD), (2 * HD, 3 * HD)],
        [(HD, 2 * HD), (3 * HD, 4 * HD)],
    )

    grad_key_turned = turned(key_sum, cosines, -sines)
    grad_gkey = jnp.sum(grad_key_turned * key_unit, axis=0, keepdims=True)
    grad_key_raw = norm_back(grad_key_turned, g_key, key_unit, key_inverse).astype(BF)
    grad_kv_raw = jnp.concatenate([grad_key_raw, value_sum.astype(BF)], axis=1)
    grad_normed_part = product_rt(
        jnp.concatenate([grad_query_wide, grad_kv_raw], axis=1),
        jnp.concatenate([w_qo[:, :HD], w_qo_other[:, :HD], w_kv], axis=1),
    )
    grad_normed = pairs_sum(grad_normed_part)
    grad_ginput = jnp.sum(grad_normed_part * input_unit, axis=0, keepdims=True)
    tokens_own = grad_middle + norm_back(grad_normed, g_input, input_unit, input_inverse)
    tokens_grad = ordered(core, tokens_own, over_core(tokens_own))

    lanes = 2 * HD

    def spread(vector, count):
        parts = vector.reshape(dp_count, 1, count)
        return jnp.pad(parts, ((0, 0), (0, 0), (0, lanes - count)))

    once = jnp.where(pair == 0, 1.0, 0.0).astype(F32)
    gain_rows = jnp.concatenate(
        [
            spread(grad_ginput, shard),
            spread(grad_gattention * once, shard),
            spread(grad_gprefeed * once, shard),
            spread(grad_gfeed * once, shard),
            spread(grad_gquery, head_shard),
            spread(grad_gkey, head_shard),
            jnp.zeros((dp_count, 10, lanes), F32),
        ],
        axis=1,
    )
    small = jnp.concatenate(
        [product_lt(normed, grad_kv_raw).reshape(dp_count, shard, lanes), gain_rows], axis=1
    ).reshape(dp_count * (shard + 16), lanes)
    columns = lanes // 2
    small = lax.dynamic_slice_in_dim(small, core * columns, columns, 1) + over_core(
        low(lax.dynamic_slice_in_dim(small, (1 - core) * columns, columns, 1))
    ).astype(F32)
    columns = columns // 2
    small = lax.dynamic_slice_in_dim(small, pair * columns, columns, 1) + over_pairs(
        low(lax.dynamic_slice_in_dim(small, (1 - pair) * columns, columns, 1))
    ).astype(F32)
    small = low(context_sum_small(dp_scattered(small)))
    other = over_pairs(small)
    small = jnp.where(
        pair == 0,
        jnp.concatenate([small, other], axis=1),
        jnp.concatenate([other, small], axis=1),
    )
    other = over_core(small)
    small = jnp.where(
        core == 0,
        jnp.concatenate([small, other], axis=1),
        jnp.concatenate([other, small], axis=1),
    ).astype(F32)

    return (
        layer_out,
        tokens_grad,
        small[shard, :shard],
        total_qo[:, :HD],
        small[:shard, :HD],
        small[:shard, HD:],
        small[shard + 4, :head_shard],
        small[shard + 5, :head_shard],
        total_qo[:, HD:].T,
        small[shard + 1, :shard],
        small[shard + 2, :shard],
        total_gate_up[:, :feed_width],
        total_gate_up[:, feed_width:],
        total_down.T,
        small[shard + 3, :shard],
    )


def solution(mesh):
    placed = (
        P(("dp", "context"), None),
        P("dp", None),
        P("dp"),
        P("dp", "tensor"),
        P("dp", None),
        P("dp", None),
        P("dp"),
        P("dp"),
        P("tensor", "dp"),
        P("dp"),
        P("dp"),
        P("dp", "tensor"),
        P("dp", "tensor"),
        P("tensor", "dp"),
        P("dp"),
        P(("dp", "context"), None),
    )
    return jax.shard_map(
        local,
        mesh=mesh,
        in_specs=placed,
        out_specs=(
            P(("dp", "context"), None),
            P(("dp", "context"), None),
            P("dp"),
            P("dp", "tensor"),
            P("dp", None),
            P("dp", None),
            P("dp"),
            P("dp"),
            P("tensor", "dp"),
            P("dp"),
            P("dp"),
            P("dp", "tensor"),
            P("dp", "tensor"),
            P("tensor", "dp"),
            P("dp"),
        ),
        check_vma=False,
    )
```

```python
import math

import jax
import jax.numpy as jnp
from jax import lax
from jax.sharding import PartitionSpec as P

HD = 256
LMAX = 2048
EPS = 1e-06
SCALE = 0.0625

BF = jnp.bfloat16
F32 = jnp.float32


def product(left_side, right_side):
    return jnp.dot(left_side, right_side, preferred_element_type=F32)


def product_lt(left_side, right_side):
    return lax.dot_general(
        left_side, right_side, (((0,), (0,)), ((), ())), preferred_element_type=F32
    )


def product_rt(left_side, right_side):
    return lax.dot_general(
        left_side, right_side, (((1,), (1,)), ((), ())), preferred_element_type=F32
    )


def low(values):
    return lax.reduce_precision(values, 8, 7).astype(BF)


def over_core(array):
    devices = lax.axis_size("tensor")
    return lax.ppermute(array, "tensor", [(i, i ^ 1) for i in range(devices)])


def over_pairs(array):
    devices = lax.axis_size("tensor")
    return lax.ppermute(array, "tensor", [(i, i ^ 2) for i in range(devices)])


def over_context(array, by):
    devices = lax.axis_size("context")
    pairs = [(i, i + by) for i in range(devices) if 0 <= i + by < devices]
    return lax.ppermute(array, "context", pairs)


def after(array, earlier):
    return lax.optimization_barrier((array, earlier))[0]


def ordered(place, mine, other, axis=0):
    first = place == 0
    return jnp.concatenate(
        [jnp.where(first, mine, other), jnp.where(first, other, mine)], axis=axis
    )


def pairs_sum(partial, meanwhile=None):
    short = low(partial)
    other = over_pairs(short)
    if meanwhile is not None:
        other = after(other, meanwhile)
    return short.astype(F32) + other.astype(F32)


def stacked_rows(vectors, rows, lanes):
    place = lax.broadcasted_iota(jnp.int32, (rows, lanes), 0)
    total = jnp.zeros((rows, lanes), vectors[0].dtype)
    for number, vector in enumerate(vectors):
        wide = jnp.pad(vector.reshape(1, -1), ((0, 0), (0, lanes - vector.size)))
        total = jnp.where(place == number, wide, total)
    return total


def dp_gathered(array):
    if lax.axis_size("dp") == 2:
        other = lax.ppermute(array, "dp", [(0, 1), (1, 0)])
        return ordered(lax.axis_index("dp"), array, other)
    return lax.all_gather(array, "dp", axis=0, tiled=True)


def dp_scattered(total):
    if lax.axis_size("dp") == 2:
        place = lax.axis_index("dp")
        rows = total.shape[0] // 2
        keep = lax.dynamic_slice_in_dim(total, place * rows, rows, 0)
        send = lax.dynamic_slice_in_dim(total, (1 - place) * rows, rows, 0)
        return keep.astype(F32) + lax.ppermute(low(send), "dp", [(0, 1), (1, 0)]).astype(F32)
    return lax.psum_scatter(low(total), "dp", scatter_dimension=0, tiled=True).astype(F32)


def context_sum(total):
    if lax.axis_size("context") != 4:
        return lax.psum(total, "context")
    place = lax.axis_index("context")
    near, far = place % 2, place // 2
    rows = total.shape[0] // 2
    keep = lax.dynamic_slice_in_dim(total, near * rows, rows, 0)
    send = lax.dynamic_slice_in_dim(total, (1 - near) * rows, rows, 0)
    by_near = [(i, i ^ 1) for i in range(4)]
    by_far = [(i, i ^ 2) for i in range(4)]
    part = keep + lax.ppermute(low(send), "context", by_near).astype(F32)
    rows = rows // 2
    keep = lax.dynamic_slice_in_dim(part, far * rows, rows, 0)
    send = lax.dynamic_slice_in_dim(part, (1 - far) * rows, rows, 0)
    part = low(keep + lax.ppermute(low(send), "context", by_far).astype(F32))
    part = ordered(far, part, lax.ppermute(part, "context", by_far))
    return ordered(near, part, lax.ppermute(part, "context", by_near)).astype(F32)


def context_sum_small(total):
    if lax.axis_size("context") != 4:
        return lax.psum(total, "context")
    for bit in (1, 2):
        short = low(total)
        other = lax.ppermute(short, "context", [(i, i ^ bit) for i in range(4)])
        total = short.astype(F32) + other.astype(F32)
    return total


def normed_of(values):
    inverse = lax.rsqrt(jnp.mean(values * values, axis=-1, keepdims=True) + EPS)
    return values * inverse, inverse


def norm_back(grad, gain, unit, inverse):
    scaled = grad * gain
    return inverse * (scaled - unit * jnp.mean(scaled * unit, axis=-1, keepdims=True))


def turned(values, cosines, sines):
    half_width = values.shape[-1] // 2
    first_half = values[..., :half_width]
    second_half = values[..., half_width:]
    return jnp.concatenate(
        [first_half * cosines - second_half * sines, second_half * cosines + first_half * sines],
        axis=-1,
    )


def local(
    tokens,
    seq_lengths,
    input_gain,
    query_weight,
    key_weight,
    value_weight,
    query_gain,
    key_gain,
    output_weight,
    attention_gain,
    prefeed_gain,
    gate_weight,
    up_weight,
    down_weight,
    feed_gain,
    cotangent,
):
    block_rows = tokens.shape[0]
    rows = block_rows // 2
    width = tokens.shape[1]
    context_place = lax.axis_index("context")
    core = lax.axis_index("tensor") % 2
    pair = lax.axis_index("tensor") // 2
    reach = min(lax.axis_size("context") - 1, (LMAX - 2) // block_rows + 1)
    dp_count = lax.axis_size("dp")
    shard = width // dp_count
    feed_width = gate_weight.shape[1]

    lanes = 2 * HD
    head_shard = HD // dp_count
    gains = [input_gain, attention_gain, prefeed_gain, feed_gain, query_gain, key_gain]
    kv_pack = jnp.concatenate(
        [
            jnp.concatenate([key_weight, value_weight], axis=1),
            stacked_rows(gains, 16, lanes),
        ],
        axis=0,
    )
    qo_pack = jnp.concatenate([query_weight, output_weight.T], axis=1)
    feed_pack = jnp.concatenate([gate_weight, up_weight, down_weight.T], axis=1)
    kv_parts = dp_gathered(kv_pack).reshape(dp_count, shard + 16, lanes)
    w_kv = kv_parts[:, :shard].reshape(width, lanes)
    w_qo = dp_gathered(after(qo_pack, w_kv))
    w_feed = dp_gathered(after(feed_pack, w_qo))
    w_qo_other = over_core(w_qo)
    w_feed_other = over_core(w_feed)

    def gain_of(number, count):
        return kv_parts[:, shard + number, :count].reshape(1, -1).astype(F32)

    g_input, g_attention, g_prefeed, g_feed = (gain_of(i, shard) for i in range(4))
    g_query, g_key = (gain_of(i, head_shard) for i in (4, 5))

    stream = lax.dynamic_slice_in_dim(tokens, core * rows, rows, 0).astype(F32)
    grad_out = lax.dynamic_slice_in_dim(cotangent, core * rows, rows, 0).astype(F32)
    row_index = (
        context_place * block_rows + core * rows + lax.broadcasted_iota(jnp.int32, (rows, 1), 0)
    )
    start = jnp.zeros_like(row_index)
    begin = jnp.int32(0)
    for number in range(seq_lengths.shape[1]):
        start = jnp.where(row_index >= begin, begin, start)
        begin = begin + seq_lengths[0, number]
    frequency = jnp.exp(
        lax.broadcasted_iota(jnp.int32, (1, HD // 2), 1).astype(F32)
        * (-2.0 * math.log(1000000.0) / HD)
    )
    angles = (row_index - start).astype(F32) * frequency
    cosines, sines = lax.optimization_barrier((jnp.cos(angles), jnp.sin(angles)))
    two_cosines = jnp.concatenate([cosines, cosines], axis=0)
    two_sines = jnp.concatenate([sines, sines], axis=0)

    input_unit, input_inverse = normed_of(stream)
    normed = (input_unit * g_input).astype(BF)

    key_value_raw = product(normed, w_kv)
    key_unit, key_inverse = normed_of(key_value_raw[:, :HD])
    key_own = turned(key_unit * g_key, cosines, sines).astype(BF)
    value_own = key_value_raw[:, HD:].astype(BF)
    current = (key_own, value_own)
    arrived = [current]
    for step in range(reach):
        current = (over_context(current[0], 1), over_context(current[1], 1))
        arrived.append(current)

    query_raw = jnp.concatenate(
        [product(normed, w_qo[:, :HD]), product(normed, w_qo_other[:, :HD])], axis=0
    )
    query_unit, query_inverse = normed_of(query_raw)
    query = turned(query_unit * g_query, two_cosines, two_sines).astype(BF)

    two_rows = jnp.concatenate([row_index, row_index], axis=0)
    two_starts = jnp.concatenate([start, start], axis=0)
    within = lax.broadcasted_iota(jnp.int32, (1, rows), 1)
    key_rows = jnp.concatenate([core * rows + within, (1 - core) * rows + within], axis=1)
    w_output = jnp.concatenate([w_qo[:, HD:], w_qo_other[:, HD:]], axis=1)
    w_gate_up = jnp.concatenate(
        [
            w_feed[:, :feed_width],
            w_feed_other[:, :feed_width],
            w_feed[:, feed_width : 2 * feed_width],
            w_feed_other[:, feed_width : 2 * feed_width],
        ],
        axis=1,
    )
    w_down = jnp.concatenate([w_feed[:, 2 * feed_width :], w_feed_other[:, 2 * feed_width :]], axis=1)
    blocks = []
    kept = []
    mass = jnp.zeros((2 * rows, 1), F32)
    heads_sum = jnp.zeros((2 * rows, HD), F32)
    for step in range(reach + 1):
        both = jnp.concatenate(arrived[step], axis=1)
        if step > 0:
            both = after(both, (mass, heads_sum))
        if step == reach:
            both = after(both, (w_output, w_gate_up, w_down))
        both = jnp.concatenate([both, over_core(both)], axis=0)
        key_block, value_block = both[:, :HD], both[:, HD:]
        blocks.append((key_block, value_block))
        key_index = (context_place - step) * block_rows + key_rows
        allowed = (key_index >= two_starts) & (key_index <= two_rows)
        weights = jnp.where(allowed, jnp.exp(product_rt(query, key_block) * SCALE), 0.0)
        mass = mass + jnp.sum(weights, axis=1, keepdims=True)
        weights = weights.astype(BF)
        heads_sum = heads_sum + product(weights, value_block)
        kept.append(weights)
    inverse_mass = 1.0 / mass
    heads = heads_sum * inverse_mass
    heads_low = heads.astype(BF)
    heads_wide = jnp.concatenate([heads_low[:rows], heads_low[rows:]], axis=1)
    attn_sum = pairs_sum(product_rt(heads_wide, w_output))

    attn_unit, attn_inverse = normed_of(attn_sum)
    middle = stream + attn_unit * g_attention
    middle_unit, middle_inverse = normed_of(middle)
    normed_feed = (middle_unit * g_prefeed).astype(BF)
    gate_up = product(normed_feed, w_gate_up)
    activation, activation_back = jax.vjp(
        lambda gate_part, up_part: jax.nn.gelu(gate_part, approximate=True) * up_part,
        gate_up[:, : 2 * feed_width],
        gate_up[:, 2 * feed_width :],
    )
    hidden = activation.astype(BF)
    feed_sum = pairs_sum(product_rt(hidden, w_down))
    feed_unit, feed_inverse = normed_of(feed_sum)
    layer_own = low(middle + feed_unit * g_feed)
    layer_out = ordered(core, layer_own, over_core(layer_own))

    grad_gfeed = jnp.sum(grad_out * feed_unit, axis=0, keepdims=True)
    grad_feed = norm_back(grad_out, g_feed, feed_unit, feed_inverse).astype(BF)
    grad_gate_full, grad_up_full = activation_back(product(grad_feed, w_down))
    grad_gate_up = jnp.concatenate([grad_gate_full.astype(BF), grad_up_full.astype(BF)], axis=1)
    def shared(total, own, other):
        mine = jnp.concatenate([total[:, a:b] for a, b in own], axis=1)
        theirs = jnp.concatenate([total[:, a:b] for a, b in other], axis=1)
        return mine, low(theirs)

    def whole(mine, theirs):
        return context_sum(dp_scattered(mine + over_core(theirs).astype(F32)))

    parts_down = shared(
        product_lt(grad_feed, hidden), [(0, feed_width)], [(feed_width, 2 * feed_width)]
    )
    parts_gate_up = shared(
        product_lt(normed_feed, grad_gate_up),
        [(0, feed_width), (2 * feed_width, 3 * feed_width)],
        [(feed_width, 2 * feed_width), (3 * feed_width, 4 * feed_width)],
    )
    grad_normed_feed = pairs_sum(
        product_rt(grad_gate_up, w_gate_up), (parts_down, parts_gate_up, layer_out)
    )
    total_down = whole(*parts_down)
    total_gate_up = whole(*parts_gate_up)

    grad_gprefeed = jnp.sum(grad_normed_feed * middle_unit, axis=0, keepdims=True)
    grad_middle = grad_out + norm_back(grad_normed_feed, g_prefeed, middle_unit, middle_inverse)
    grad_gattention = jnp.sum(grad_middle * attn_unit, axis=0, keepdims=True)
    grad_attn = norm_back(grad_middle, g_attention, attn_unit, attn_inverse).astype(BF)

    grad_heads_wide = product(grad_attn, w_output)
    grad_heads = jnp.concatenate([grad_heads_wide[:, :HD], grad_heads_wide[:, HD:]], axis=0)
    grad_heads_low = (grad_heads * inverse_mass).astype(BF)
    row_dots = jnp.sum(grad_heads * heads, axis=1, keepdims=True) * inverse_mass
    grad_query = jnp.zeros((2 * rows, HD), F32)
    piece = rows // 2
    piece_sums = []
    for step in range(reach, -1, -1):
        key_block, value_block = blocks[step]
        weights = kept[step]
        grad_scores = (
            weights.astype(F32) * (product_rt(grad_heads_low, value_block) - row_dots)
        ).astype(BF)
        both = jnp.concatenate(
            [product_lt(grad_scores, query) * SCALE, product_lt(weights, grad_heads_low)], axis=1
        )
        both = both[:rows] + over_core(low(both[rows:])).astype(F32)
        keep = lax.dynamic_slice_in_dim(both, pair * piece, piece, 0)
        send = lax.dynamic_slice_in_dim(both, (1 - pair) * piece, piece, 0)
        both = keep + over_pairs(low(send)).astype(F32)
        if step > 0:
            both = over_context(low(both), -step).astype(F32)
        piece_sums.append(both)
        grad_query = grad_query + product(grad_scores, key_block)
    grad_kv = sum(piece_sums[1:], piece_sums[0])

    grad_query_turned = turned(grad_query * SCALE, two_cosines, -two_sines)
    grad_gquery = jnp.sum(grad_query_turned * query_unit, axis=0, keepdims=True)
    grad_query_raw = norm_back(grad_query_turned, g_query, query_unit, query_inverse).astype(BF)
    grad_query_wide = jnp.concatenate([grad_query_raw[:rows], grad_query_raw[rows:]], axis=1)
    grad_normed_query = product_rt(
        grad_query_wide, jnp.concatenate([w_qo[:, :HD], w_qo_other[:, :HD]], axis=1)
    )
    parts_qo = shared(
        jnp.concatenate(
            [product_lt(normed, grad_query_wide), product_lt(grad_attn, heads_wide)], axis=1
        ),
        [(0, HD), (2 * HD, 3 * HD)],
        [(HD, 2 * HD), (3 * HD, 4 * HD)],
    )
    grad_normed = pairs_sum(grad_normed_query, parts_qo)
    total_qo = whole(*parts_qo)

    def piece_of(array):
        return lax.dynamic_slice_in_dim(array, pair * piece, piece, 0)

    piece_unit = piece_of(key_unit)
    grad_key_turned = turned(grad_kv[:, :HD], piece_of(cosines), -piece_of(sines))
    grad_gkey = jnp.sum(grad_key_turned * piece_unit, axis=0, keepdims=True)
    grad_key_raw = norm_back(grad_key_turned, g_key, piece_unit, piece_of(key_inverse)).astype(BF)
    grad_kv_raw = jnp.concatenate([grad_key_raw, grad_kv[:, HD:].astype(BF)], axis=1)
    grad_normed_kv = low(product_rt(grad_kv_raw, w_kv))
    grad_ginput = jnp.sum(grad_normed_query * input_unit, axis=0, keepdims=True) + jnp.sum(
        grad_normed_kv.astype(F32) * piece_of(input_unit), axis=0, keepdims=True
    )

    once = jnp.where(pair == 0, 1.0, 0.0).astype(F32)
    gain_grads = [
        (grad_ginput, shard),
        (grad_gattention * once, shard),
        (grad_gprefeed * once, shard),
        (grad_gfeed * once, shard),
        (grad_gquery, head_shard),
        (grad_gkey, head_shard),
    ]
    grad_w_kv = product_lt(piece_of(normed), grad_kv_raw)
    small = jnp.concatenate(
        [
            part
            for i in range(dp_count)
            for part in (
                grad_w_kv[i * shard : (i + 1) * shard],
                stacked_rows([g[:, i * n : (i + 1) * n] for g, n in gain_grads], 16, lanes),
            )
        ],
        axis=0,
    )
    columns = lanes // 2
    small = lax.dynamic_slice_in_dim(small, core * columns, columns, 1) + over_core(
        low(lax.dynamic_slice_in_dim(small, (1 - core) * columns, columns, 1))
    ).astype(F32)
    columns = columns // 2
    small = lax.dynamic_slice_in_dim(small, pair * columns, columns, 1) + over_pairs(
        low(lax.dynamic_slice_in_dim(small, (1 - pair) * columns, columns, 1))
    ).astype(F32)
    other = over_pairs(grad_normed_kv)
    grad_normed = grad_normed + ordered(pair, grad_normed_kv, other).astype(F32)
    tokens_own = grad_middle + norm_back(grad_normed, g_input, input_unit, input_inverse)
    tokens_grad = ordered(core, tokens_own, over_core(tokens_own))
    small = low(context_sum_small(dp_scattered(small)))
    small = ordered(pair, small, over_pairs(small), axis=1)
    small = ordered(core, small, over_core(small), axis=1).astype(F32)

    return (
        layer_out,
        tokens_grad,
        small[shard, :shard],
        total_qo[:, :HD],
        small[:shard, :HD],
        small[:shard, HD:],
        small[shard + 4, :head_shard],
        small[shard + 5, :head_shard],
        total_qo[:, HD:].T,
        small[shard + 1, :shard],
        small[shard + 2, :shard],
        total_gate_up[:, :feed_width],
        total_gate_up[:, feed_width:],
        total_down.T,
        small[shard + 3, :shard],
    )


def solution(mesh):
    placed = (
        P(("dp", "context"), None),
        P("dp", None),
        P("dp"),
        P("dp", "tensor"),
        P("dp", None),
        P("dp", None),
        P("dp"),
        P("dp"),
        P("tensor", "dp"),
        P("dp"),
        P("dp"),
        P("dp", "tensor"),
        P("dp", "tensor"),
        P("tensor", "dp"),
        P("dp"),
        P(("dp", "context"), None),
    )
    return jax.shard_map(
        local,
        mesh=mesh,
        in_specs=placed,
        out_specs=(
            P(("dp", "context"), None),
            P(("dp", "context"), None),
            P("dp"),
            P("dp", "tensor"),
            P("dp", None),
            P("dp", None),
            P("dp"),
            P("dp"),
            P("tensor", "dp"),
            P("dp"),
            P("dp"),
            P("dp", "tensor"),
            P("dp", "tensor"),
            P("tensor", "dp"),
            P("dp"),
        ),
        check_vma=False,
    )
```

```python
import math

import jax
import jax.numpy as jnp
from jax import lax
from jax.sharding import PartitionSpec as P

HD = 256
LMAX = 2048
EPS = 1e-06
SCALE = 0.0625

BF = jnp.bfloat16
F32 = jnp.float32


def product(left_side, right_side):
    return jnp.dot(left_side, right_side, preferred_element_type=F32)


def product_lt(left_side, right_side):
    return lax.dot_general(
        left_side, right_side, (((0,), (0,)), ((), ())), preferred_element_type=F32
    )


def product_rt(left_side, right_side):
    return lax.dot_general(
        left_side, right_side, (((1,), (1,)), ((), ())), preferred_element_type=F32
    )


def low(values):
    return lax.reduce_precision(values, 8, 7).astype(BF)


def over_core(array):
    devices = lax.axis_size("tensor")
    return lax.ppermute(array, "tensor", [(i, i ^ 1) for i in range(devices)])


def over_pairs(array):
    devices = lax.axis_size("tensor")
    return lax.ppermute(array, "tensor", [(i, i ^ 2) for i in range(devices)])


def over_context(array, by):
    devices = lax.axis_size("context")
    pairs = [(i, i + by) for i in range(devices) if 0 <= i + by < devices]
    return lax.ppermute(array, "context", pairs)


def after(array, earlier):
    return lax.optimization_barrier((array, earlier))[0]


def ordered(place, mine, other, axis=0):
    first = place == 0
    return jnp.concatenate(
        [jnp.where(first, mine, other), jnp.where(first, other, mine)], axis=axis
    )


def pairs_sum(partial, meanwhile=None):
    short = low(partial)
    other = over_pairs(short)
    if meanwhile is not None:
        other = after(other, meanwhile)
    return short.astype(F32) + other.astype(F32)


def stacked_rows(vectors, rows):
    lanes = vectors[0].size
    place = lax.broadcasted_iota(jnp.int32, (rows, lanes), 0)
    total = jnp.zeros((rows, lanes), vectors[0].dtype)
    for number, vector in enumerate(vectors):
        wide = lax.broadcast_in_dim(vector.reshape(-1), (rows, lanes), (1,))
        total = jnp.where(place == number, wide, total)
    return total


def dp_gathered(array, axis=0):
    if lax.axis_size("dp") == 2:
        other = lax.ppermute(array, "dp", [(0, 1), (1, 0)])
        return ordered(lax.axis_index("dp"), array, other, axis)
    return lax.all_gather(array, "dp", axis=axis, tiled=True)


def dp_scattered(total):
    if lax.axis_size("dp") == 2:
        place = lax.axis_index("dp")
        rows = total.shape[0] // 2
        keep = lax.dynamic_slice_in_dim(total, place * rows, rows, 0)
        send = lax.dynamic_slice_in_dim(total, (1 - place) * rows, rows, 0)
        return keep.astype(F32) + lax.ppermute(low(send), "dp", [(0, 1), (1, 0)]).astype(F32)
    return lax.psum_scatter(low(total), "dp", scatter_dimension=0, tiled=True).astype(F32)


def sum_near(total):
    if lax.axis_size("context") != 4:
        return lax.psum(low(total), "context")
    near = lax.axis_index("context") % 2
    rows = total.shape[0] // 2
    keep = lax.dynamic_slice_in_dim(total, near * rows, rows, 0)
    send = lax.dynamic_slice_in_dim(total, (1 - near) * rows, rows, 0)
    return keep + lax.ppermute(low(send), "context", [(i, i ^ 1) for i in range(4)]).astype(F32)


def sum_far(part):
    if lax.axis_size("context") != 4:
        return part
    far = lax.axis_index("context") // 2
    rows = part.shape[0] // 2
    keep = lax.dynamic_slice_in_dim(part, far * rows, rows, 0)
    send = lax.dynamic_slice_in_dim(part, (1 - far) * rows, rows, 0)
    return low(keep + lax.ppermute(low(send), "context", [(i, i ^ 2) for i in range(4)]).astype(F32))


def spread_far(part):
    if lax.axis_size("context") != 4:
        return part
    other = lax.ppermute(part, "context", [(i, i ^ 2) for i in range(4)])
    return ordered(lax.axis_index("context") // 2, part, other)


def spread_near(part):
    if lax.axis_size("context") != 4:
        return part.astype(F32)
    other = lax.ppermute(part, "context", [(i, i ^ 1) for i in range(4)])
    return ordered(lax.axis_index("context") % 2, part, other).astype(F32)


def context_sum_small(total):
    if lax.axis_size("context") != 4:
        return lax.psum(total, "context")
    short = low(total)
    other = [
        lax.ppermute(short, "context", [(i, (i + by) % 4) for i in range(4)]).astype(F32)
        for by in (1, 2, 3)
    ]
    return (short.astype(F32) + other[1]) + (other[0] + other[2])


def partner(array, dp_turn, tensor_turn):
    count = lax.axis_size("tensor")
    pairs = [
        (i * count + j, (i ^ dp_turn) * count + (j ^ tensor_turn))
        for i in range(lax.axis_size("dp"))
        for j in range(count)
    ]
    return lax.ppermute(array, ("dp", "tensor"), pairs)


def owners_sum(total, columns):
    place = lax.axis_index("dp")
    pair = lax.axis_index("tensor") // 2
    rows = total.shape[0] // lax.axis_size("dp")
    if lax.axis_size("dp") != 2:
        total = lax.dynamic_slice_in_dim(total, pair * columns, columns, 1) + over_pairs(
            low(lax.dynamic_slice_in_dim(total, (1 - pair) * columns, columns, 1))
        ).astype(F32)
        return dp_scattered(total)

    def part(dp_turn, pair_turn):
        at = (jnp.bitwise_xor(place, dp_turn) * rows, jnp.bitwise_xor(pair, pair_turn) * columns)
        return lax.dynamic_slice(total, at, (rows, columns))

    whole = part(0, 0)
    for dp_turn, pair_turn in ((0, 1), (1, 0), (1, 1)):
        short = low(part(dp_turn, pair_turn))
        whole = whole + partner(short, dp_turn, 2 * pair_turn).astype(F32)
    return whole


def normed_of(values):
    inverse = lax.rsqrt(jnp.mean(values * values, axis=-1, keepdims=True) + EPS)
    return values * inverse, inverse


def norm_back(grad, gain, unit, inverse):
    scaled = grad * gain
    return inverse * (scaled - unit * jnp.mean(scaled * unit, axis=-1, keepdims=True))


def turned(values, cosines, sines):
    half_width = values.shape[-1] // 2
    first_half = values[..., :half_width]
    second_half = values[..., half_width:]
    return jnp.concatenate(
        [first_half * cosines - second_half * sines, second_half * cosines + first_half * sines],
        axis=-1,
    )


def local(
    tokens,
    seq_lengths,
    input_gain,
    query_weight,
    key_weight,
    value_weight,
    query_gain,
    key_gain,
    output_weight,
    attention_gain,
    prefeed_gain,
    gate_weight,
    up_weight,
    down_weight,
    feed_gain,
    cotangent,
):
    block_rows = tokens.shape[0]
    rows = block_rows // 2
    width = tokens.shape[1]
    context_place = lax.axis_index("context")
    core = lax.axis_index("tensor") % 2
    pair = lax.axis_index("tensor") // 2
    reach = min(lax.axis_size("context") - 1, (LMAX - 2) // block_rows + 1)
    dp_count = lax.axis_size("dp")
    shard = width // dp_count
    feed_width = gate_weight.shape[1]

    lanes = 2 * HD
    head_shard = HD // dp_count
    gains = jnp.concatenate(
        [
            stacked_rows([input_gain, attention_gain, prefeed_gain, feed_gain], 16),
            stacked_rows([query_gain, key_gain], 16),
        ],
        axis=1,
    )
    w_key = dp_gathered(key_weight)
    w_value = dp_gathered(value_weight)
    gain_parts = dp_gathered(gains).reshape(dp_count, 16, shard + head_shard)
    query_weight, output_weight = after((query_weight, output_weight), (w_key, w_value))
    w_query = dp_gathered(query_weight)
    w_out = dp_gathered(output_weight, axis=1)
    gate_weight, up_weight, down_weight = after(
        (gate_weight, up_weight, down_weight), (w_query, w_out)
    )
    w_gate, w_up, w_down = lax.optimization_barrier(
        (dp_gathered(gate_weight), dp_gathered(up_weight), dp_gathered(down_weight.T))
    )
    w_query_two = jnp.concatenate([w_query, over_core(w_query)], axis=1)
    w_output = jnp.concatenate([w_out, over_core(w_out)], axis=0)
    w_gate_up = jnp.concatenate([w_gate, over_core(w_gate), w_up, over_core(w_up)], axis=1)
    w_down = jnp.concatenate([w_down, over_core(w_down)], axis=1)

    def gain_of(number, first, count):
        return gain_parts[:, number, first : first + count].reshape(1, -1).astype(F32)

    g_input, g_attention, g_prefeed, g_feed = (gain_of(i, 0, shard) for i in range(4))
    g_query, g_key = (gain_of(i, shard, head_shard) for i in (0, 1))

    stream = lax.dynamic_slice_in_dim(tokens, core * rows, rows, 0).astype(F32)
    grad_out = lax.dynamic_slice_in_dim(cotangent, core * rows, rows, 0).astype(F32)
    row_index = (
        context_place * block_rows + core * rows + lax.broadcasted_iota(jnp.int32, (rows, 1), 0)
    )
    start = jnp.zeros_like(row_index)
    begin = jnp.int32(0)
    for number in range(seq_lengths.shape[1]):
        start = jnp.where(row_index >= begin, begin, start)
        begin = begin + seq_lengths[0, number]
    frequency = jnp.exp(
        lax.broadcasted_iota(jnp.int32, (1, HD // 2), 1).astype(F32)
        * (-2.0 * math.log(1000000.0) / HD)
    )
    angles = (row_index - start).astype(F32) * frequency
    cosines, sines = lax.optimization_barrier((jnp.cos(angles), jnp.sin(angles)))
    two_cosines = jnp.concatenate([cosines, cosines], axis=0)
    two_sines = jnp.concatenate([sines, sines], axis=0)

    input_unit, input_inverse = normed_of(stream)
    normed = (input_unit * g_input).astype(BF)

    w_kv = jnp.concatenate([w_key, w_value], axis=1)
    key_value_raw = product(normed, w_kv)
    key_unit, key_inverse = normed_of(key_value_raw[:, :HD])
    kv_own = jnp.concatenate(
        [
            turned(key_unit * g_key, cosines, sines).astype(BF),
            key_value_raw[:, HD:].astype(BF),
        ],
        axis=1,
    )
    piece = rows // 2

    def piece_of(array, own=True):
        return lax.dynamic_slice_in_dim(array, (pair if own else 1 - pair) * piece, piece, 0)

    current = (kv_own[:, :HD], kv_own[:, HD:])
    arrived = [kv_own]
    for step in range(reach):
        current = (over_context(current[0], 1), over_context(current[1], 1))
        arrived.append(jnp.concatenate(current, axis=1))

    query_raw = product(normed, w_query_two)
    query_raw = jnp.concatenate([query_raw[:, :HD], query_raw[:, HD:]], axis=0)
    query_unit, query_inverse = normed_of(query_raw)
    query = turned(query_unit * g_query, two_cosines, two_sines).astype(BF)

    two_rows = jnp.concatenate([row_index, row_index], axis=0)
    two_starts = jnp.concatenate([start, start], axis=0)
    within = lax.broadcasted_iota(jnp.int32, (1, rows), 1)
    key_rows = jnp.concatenate([core * rows + within, (1 - core) * rows + within], axis=1)
    blocks = []
    kept = []
    mass = jnp.zeros((2 * rows, 1), F32)
    heads_sum = jnp.zeros((2 * rows, HD), F32)
    for step in range(reach + 1):
        both = arrived[step]
        if step == reach:
            both = after(both, (mass, heads_sum, w_gate_up, w_down))
        both = jnp.concatenate([both, over_core(both)], axis=0)
        key_block, value_block = both[:, :HD], both[:, HD:]
        blocks.append((key_block, value_block))
        key_index = (context_place - step) * block_rows + key_rows
        allowed = (key_index >= two_starts) & (key_index <= two_rows)
        weights = jnp.where(allowed, jnp.exp(product_rt(query, key_block) * SCALE), 0.0)
        mass = mass + jnp.sum(weights, axis=1, keepdims=True)
        weights = weights.astype(BF)
        heads_sum = heads_sum + product(weights, value_block)
        kept.append(weights)
    inverse_mass = 1.0 / mass
    heads = heads_sum * inverse_mass
    heads_low = heads.astype(BF)
    heads_wide = jnp.concatenate([heads_low[:rows], heads_low[rows:]], axis=1)
    attn_sum = pairs_sum(product(heads_wide, w_output))

    attn_unit, attn_inverse = normed_of(attn_sum)
    middle = stream + attn_unit * g_attention
    middle_unit, middle_inverse = normed_of(middle)
    normed_feed = (middle_unit * g_prefeed).astype(BF)
    gate_up = product(normed_feed, w_gate_up)
    activation, activation_back = jax.vjp(
        lambda gate_part, up_part: jax.nn.gelu(gate_part, approximate=True) * up_part,
        gate_up[:, : 2 * feed_width],
        gate_up[:, 2 * feed_width :],
    )
    hidden = activation.astype(BF)
    feed_sum = pairs_sum(product_rt(hidden, w_down))
    feed_unit, feed_inverse = normed_of(feed_sum)
    layer_own = low(middle + feed_unit * g_feed)
    layer_out = ordered(core, layer_own, over_core(layer_own))

    grad_gfeed = jnp.sum(grad_out * feed_unit, axis=0, keepdims=True)
    grad_feed = norm_back(grad_out, g_feed, feed_unit, feed_inverse).astype(BF)
    grad_gate_full, grad_up_full = activation_back(product(grad_feed, w_down))
    grad_gate_up = jnp.concatenate([grad_gate_full.astype(BF), grad_up_full.astype(BF)], axis=1)
    def shared(total, own, other):
        mine = jnp.concatenate([total[:, a:b] for a, b in own], axis=1)
        theirs = jnp.concatenate([total[:, a:b] for a, b in other], axis=1)
        return mine, low(theirs)

    parts_down = shared(
        product_lt(grad_feed, hidden), [(0, feed_width)], [(feed_width, 2 * feed_width)]
    )
    whole_down = parts_down[0] + over_core(parts_down[1]).astype(F32)
    feed_part = low(product_rt(grad_gate_up, w_gate_up))
    feed_other = over_pairs(feed_part)
    parts_gate_up = shared(
        product_lt(*after((normed_feed, grad_gate_up), feed_part)),
        [(0, feed_width), (2 * feed_width, 3 * feed_width)],
        [(feed_width, 2 * feed_width), (3 * feed_width, 4 * feed_width)],
    )
    whole_gate_up = parts_gate_up[0] + over_core(parts_gate_up[1]).astype(F32)
    shard_down = dp_scattered(whole_down)
    feed_other = after(feed_other, (whole_gate_up, shard_down, layer_out))
    grad_normed_feed = feed_part.astype(F32) + feed_other.astype(F32)
    shard_gate_up = dp_scattered(whole_gate_up)
    near_down = sum_near(shard_down)

    grad_gprefeed = jnp.sum(grad_normed_feed * middle_unit, axis=0, keepdims=True)
    grad_middle = grad_out + norm_back(grad_normed_feed, g_prefeed, middle_unit, middle_inverse)
    grad_gattention = jnp.sum(grad_middle * attn_unit, axis=0, keepdims=True)
    grad_attn = norm_back(grad_middle, g_attention, attn_unit, attn_inverse).astype(BF)

    grad_heads_wide = product_rt(grad_attn, w_output)
    grad_heads = jnp.concatenate([grad_heads_wide[:, :HD], grad_heads_wide[:, HD:]], axis=0)
    grad_heads_low = (grad_heads * inverse_mass).astype(BF)
    row_dots = jnp.sum(grad_heads * heads, axis=1, keepdims=True) * inverse_mass
    grad_query = jnp.zeros((2 * rows, HD), F32)
    block_grads = {}
    for step in range(reach, -1, -1):
        key_block, value_block = blocks[step]
        weights = kept[step]
        if step == reach - 1:
            weights = after(weights, (near_down, block_grads[reach]))
            far_down = sum_far(near_down)
        if step == reach - 2:
            weights = after(weights, (far_down, block_grads[reach - 1]))
            all_down = spread_far(far_down)
        if step == 0:
            weights = after(weights, (shard_gate_up, all_down, block_grads[1]))
            near_gate_up = sum_near(shard_gate_up)
        grad_scores = (
            weights.astype(F32) * (product_rt(grad_heads_low, value_block) - row_dots)
        ).astype(BF)
        block_grads[step] = jnp.concatenate(
            [product_lt(grad_scores, query) * SCALE, product_lt(weights, grad_heads_low)], axis=1
        )
        grad_query = grad_query + product(grad_scores, key_block)
    grad_query_turned = turned(grad_query * SCALE, two_cosines, -two_sines)
    grad_gquery = jnp.sum(grad_query_turned * query_unit, axis=0, keepdims=True)
    grad_query_raw = norm_back(grad_query_turned, g_query, query_unit, query_inverse).astype(BF)
    grad_query_wide = jnp.concatenate([grad_query_raw[:rows], grad_query_raw[rows:]], axis=1)
    grad_normed_query = product_rt(grad_query_wide, w_query_two)
    parts_qo = shared(
        jnp.concatenate(
            [product_lt(normed, grad_query_wide), product_lt(grad_attn, heads_wide)], axis=1
        ),
        [(0, HD), (2 * HD, 3 * HD)],
        [(HD, 2 * HD), (3 * HD, 4 * HD)],
    )
    whole_qo = parts_qo[0] + over_core(parts_qo[1]).astype(F32)

    def group_sum(group, first_due, then_due):
        theirs = over_core(jnp.concatenate([low(block_grads[s][rows:]) for s in group], axis=0))
        if first_due is not None:
            theirs = after(theirs, first_due)
        mine = jnp.concatenate([block_grads[s][:rows] for s in group], axis=0) + theirs.astype(F32)
        mine = mine.reshape(len(group), rows, lanes)
        keep = lax.dynamic_slice_in_dim(mine, pair * piece, piece, 1)
        send = low(lax.dynamic_slice_in_dim(mine, (1 - pair) * piece, piece, 1))
        other = over_pairs(send)
        if then_due is not None:
            other = after(other, then_due)
        return keep + other.astype(F32)

    far_group = list(range(reach, 1, -1))
    near_group = [1, 0]
    far_sums = group_sum(far_group, near_gate_up, whole_qo)
    far_gate_up = sum_far(near_gate_up)
    shard_qo = dp_scattered(whole_qo)
    far_parts = [
        over_context(low(far_sums[number]), -step) for number, step in enumerate(far_group)
    ]
    near_sums = group_sum(near_group, far_gate_up, far_parts[0])
    near_part = over_context(low(near_sums[0]), -1)
    all_gate_up = spread_far(far_gate_up)
    grad_normed_query_low = low(after(grad_normed_query, near_sums))
    far_parts, near_part = after((far_parts, near_part), (shard_qo, all_gate_up))
    grad_kv = near_sums[1] + near_part.astype(F32)
    for part in far_parts:
        grad_kv = grad_kv + part.astype(F32)
    near_qo = sum_near(after(shard_qo, grad_kv))
    grad_normed = grad_normed_query_low.astype(F32) + over_pairs(grad_normed_query_low).astype(F32)

    piece_unit = piece_of(key_unit)
    grad_key_turned = turned(grad_kv[:, :HD], piece_of(cosines), -piece_of(sines))
    grad_gkey = jnp.sum(grad_key_turned * piece_unit, axis=0, keepdims=True)
    grad_key_raw = norm_back(grad_key_turned, g_key, piece_unit, piece_of(key_inverse)).astype(BF)
    grad_kv_raw = jnp.concatenate([grad_key_raw, grad_kv[:, HD:].astype(BF)], axis=1)
    grad_normed_kv = low(product_rt(grad_kv_raw, w_kv))
    grad_ginput = jnp.sum(grad_normed_query * input_unit, axis=0, keepdims=True) + jnp.sum(
        grad_normed_kv.astype(F32) * piece_of(input_unit), axis=0, keepdims=True
    )

    once = jnp.where(pair == 0, 1.0, 0.0).astype(F32)
    long_grads = [
        grad_ginput, grad_gattention * once, grad_gprefeed * once, grad_gfeed * once
    ]
    gain_rows = [
        jnp.pad(
            jnp.concatenate(
                [
                    stacked_rows([g[:, i * shard : (i + 1) * shard] for g in long_grads], 16),
                    stacked_rows(
                        [
                            g[:, i * head_shard : (i + 1) * head_shard]
                            for g in (grad_gquery, grad_gkey)
                        ],
                        16,
                    ),
                ],
                axis=1,
            ),
            ((0, 0), (0, lanes - shard - head_shard)),
        )
        for i in range(dp_count)
    ]
    grad_w_kv = product_lt(piece_of(normed), grad_kv_raw)
    small = jnp.concatenate(
        [
            part
            for i in range(dp_count)
            for part in (
                grad_w_kv[i * shard : (i + 1) * shard],
                gain_rows[i],
            )
        ],
        axis=0,
    )
    columns = lanes // 2
    other = over_core(low(lax.dynamic_slice_in_dim(small, (1 - core) * columns, columns, 1)))
    small = lax.dynamic_slice_in_dim(small, core * columns, columns, 1)
    small = small + after(other, near_qo).astype(F32)
    far_qo = sum_far(after(near_qo, small))
    small = owners_sum(small, columns // 2)
    other = over_pairs(grad_normed_kv)
    grad_normed = grad_normed + ordered(pair, grad_normed_kv, other).astype(F32)
    tokens_own = grad_middle + norm_back(grad_normed, g_input, input_unit, input_inverse)
    tokens_other = over_core(tokens_own)
    small = after(small, far_qo)
    total_gate_up = spread_near(all_gate_up)
    all_qo = spread_far(far_qo)
    small = low(context_sum_small(small))
    total_qo = spread_near(all_qo)
    total_down = spread_near(all_down)
    tokens_grad = ordered(core, tokens_own, tokens_other)
    over_both = partner(small, 0, 3)
    other_core = over_core(small)
    small = ordered(pair, small, over_pairs(small), axis=1)
    small = ordered(core, small, ordered(pair, other_core, over_both, axis=1), axis=1).astype(F32)

    return (
        layer_out,
        tokens_grad,
        small[shard, :shard],
        total_qo[:, :HD],
        small[:shard, :HD],
        small[:shard, HD:],
        small[shard, shard : shard + head_shard],
        small[shard + 1, shard : shard + head_shard],
        total_qo[:, HD:].T,
        small[shard + 1, :shard],
        small[shard + 2, :shard],
        total_gate_up[:, :feed_width],
        total_gate_up[:, feed_width:],
        total_down.T,
        small[shard + 3, :shard],
    )


def solution(mesh):
    placed = (
        P(("dp", "context"), None),
        P("dp", None),
        P("dp"),
        P("dp", "tensor"),
        P("dp", None),
        P("dp", None),
        P("dp"),
        P("dp"),
        P("tensor", "dp"),
        P("dp"),
        P("dp"),
        P("dp", "tensor"),
        P("dp", "tensor"),
        P("tensor", "dp"),
        P("dp"),
        P(("dp", "context"), None),
    )
    return jax.shard_map(
        local,
        mesh=mesh,
        in_specs=placed,
        out_specs=(
            P(("dp", "context"), None),
            P(("dp", "context"), None),
            P("dp"),
            P("dp", "tensor"),
            P("dp", None),
            P("dp", None),
            P("dp"),
            P("dp"),
            P("tensor", "dp"),
            P("dp"),
            P("dp"),
            P("dp", "tensor"),
            P("dp", "tensor"),
            P("tensor", "dp"),
            P("dp"),
        ),
        check_vma=False,
    )
```

```python
import math

import jax
import jax.numpy as jnp
from jax import lax
from jax.sharding import PartitionSpec as P

HD = 256
LMAX = 2048
EPS = 1e-06
SCALE = 0.0625

BF = jnp.bfloat16
F32 = jnp.float32


def product(left_side, right_side):
    return jnp.dot(left_side, right_side, preferred_element_type=F32)


def product_lt(left_side, right_side):
    return lax.dot_general(
        left_side, right_side, (((0,), (0,)), ((), ())), preferred_element_type=F32
    )


def product_rt(left_side, right_side):
    return lax.dot_general(
        left_side, right_side, (((1,), (1,)), ((), ())), preferred_element_type=F32
    )


def low(values):
    return lax.reduce_precision(values, 8, 7).astype(BF)


def over_core(array):
    devices = lax.axis_size("tensor")
    return lax.ppermute(array, "tensor", [(i, i ^ 1) for i in range(devices)])


def over_pairs(array):
    devices = lax.axis_size("tensor")
    return lax.ppermute(array, "tensor", [(i, i ^ 2) for i in range(devices)])


def over_context(array, by):
    devices = lax.axis_size("context")
    pairs = [(i, i + by) for i in range(devices) if 0 <= i + by < devices]
    return lax.ppermute(array, "context", pairs)


def after(array, earlier):
    return lax.optimization_barrier((array, earlier))[0]


def ordered(place, mine, other, axis=0):
    first = place == 0
    return jnp.concatenate(
        [jnp.where(first, mine, other), jnp.where(first, other, mine)], axis=axis
    )


def pairs_sum(partial, meanwhile=None):
    short = low(partial)
    other = over_pairs(short)
    if meanwhile is not None:
        other = after(other, meanwhile)
    return short.astype(F32) + other.astype(F32)


def stacked_rows(vectors, rows):
    lanes = vectors[0].size
    place = lax.broadcasted_iota(jnp.int32, (rows, lanes), 0)
    total = jnp.zeros((rows, lanes), vectors[0].dtype)
    for number, vector in enumerate(vectors):
        wide = lax.broadcast_in_dim(vector.reshape(-1), (rows, lanes), (1,))
        total = jnp.where(place == number, wide, total)
    return total


def dp_gathered(array, axis=0):
    if lax.axis_size("dp") == 2:
        other = lax.ppermute(array, "dp", [(0, 1), (1, 0)])
        return ordered(lax.axis_index("dp"), array, other, axis)
    return lax.all_gather(array, "dp", axis=axis, tiled=True)


def dp_scattered(total):
    if lax.axis_size("dp") == 2:
        place = lax.axis_index("dp")
        rows = total.shape[0] // 2
        keep = lax.dynamic_slice_in_dim(total, place * rows, rows, 0)
        send = lax.dynamic_slice_in_dim(total, (1 - place) * rows, rows, 0)
        return keep.astype(F32) + lax.ppermute(low(send), "dp", [(0, 1), (1, 0)]).astype(F32)
    return lax.psum_scatter(low(total), "dp", scatter_dimension=0, tiled=True).astype(F32)


def sum_near(total):
    if lax.axis_size("context") != 4:
        return lax.psum(low(total), "context")
    near = lax.axis_index("context") % 2
    rows = total.shape[0] // 2
    keep = lax.dynamic_slice_in_dim(total, near * rows, rows, 0)
    send = lax.dynamic_slice_in_dim(total, (1 - near) * rows, rows, 0)
    return keep + lax.ppermute(low(send), "context", [(i, i ^ 1) for i in range(4)]).astype(F32)


def sum_far(part):
    if lax.axis_size("context") != 4:
        return part
    far = lax.axis_index("context") // 2
    rows = part.shape[0] // 2
    keep = lax.dynamic_slice_in_dim(part, far * rows, rows, 0)
    send = lax.dynamic_slice_in_dim(part, (1 - far) * rows, rows, 0)
    return low(keep + lax.ppermute(low(send), "context", [(i, i ^ 2) for i in range(4)]).astype(F32))


def spread_far(part):
    if lax.axis_size("context") != 4:
        return part
    other = lax.ppermute(part, "context", [(i, i ^ 2) for i in range(4)])
    return ordered(lax.axis_index("context") // 2, part, other)


def spread_near(part):
    if lax.axis_size("context") != 4:
        return part.astype(F32)
    other = lax.ppermute(part, "context", [(i, i ^ 1) for i in range(4)])
    return ordered(lax.axis_index("context") % 2, part, other).astype(F32)


def context_sum_small(total):
    if lax.axis_size("context") != 4:
        return lax.psum(total, "context")
    short = low(total)
    other = [
        lax.ppermute(short, "context", [(i, (i + by) % 4) for i in range(4)]).astype(F32)
        for by in (1, 2, 3)
    ]
    return (short.astype(F32) + other[1]) + (other[0] + other[2])


def partner(array, dp_turn, tensor_turn):
    count = lax.axis_size("tensor")
    pairs = [
        (i * count + j, (i ^ dp_turn) * count + (j ^ tensor_turn))
        for i in range(lax.axis_size("dp"))
        for j in range(count)
    ]
    return lax.ppermute(array, ("dp", "tensor"), pairs)


def owners_sum(total, columns):
    place = lax.axis_index("dp")
    pair = lax.axis_index("tensor") // 2
    rows = total.shape[0] // lax.axis_size("dp")
    if lax.axis_size("dp") != 2:
        total = lax.dynamic_slice_in_dim(total, pair * columns, columns, 1) + over_pairs(
            low(lax.dynamic_slice_in_dim(total, (1 - pair) * columns, columns, 1))
        ).astype(F32)
        return dp_scattered(total)

    def part(dp_turn, pair_turn):
        at = (jnp.bitwise_xor(place, dp_turn) * rows, jnp.bitwise_xor(pair, pair_turn) * columns)
        return lax.dynamic_slice(total, at, (rows, columns))

    whole = part(0, 0)
    for dp_turn, pair_turn in ((0, 1), (1, 0), (1, 1)):
        short = low(part(dp_turn, pair_turn))
        whole = whole + partner(short, dp_turn, 2 * pair_turn).astype(F32)
    return whole


def normed_of(values):
    inverse = lax.rsqrt(jnp.mean(values * values, axis=-1, keepdims=True) + EPS)
    return values * inverse, inverse


def norm_back(grad, gain, unit, inverse):
    scaled = grad * gain
    return inverse * (scaled - unit * jnp.mean(scaled * unit, axis=-1, keepdims=True))


def turned(values, cosines, sines):
    half_width = values.shape[-1] // 2
    first_half = values[..., :half_width]
    second_half = values[..., half_width:]
    return jnp.concatenate(
        [first_half * cosines - second_half * sines, second_half * cosines + first_half * sines],
        axis=-1,
    )


def local(
    tokens,
    seq_lengths,
    input_gain,
    query_weight,
    key_weight,
    value_weight,
    query_gain,
    key_gain,
    output_weight,
    attention_gain,
    prefeed_gain,
    gate_weight,
    up_weight,
    down_weight,
    feed_gain,
    cotangent,
):
    block_rows = tokens.shape[0]
    rows = block_rows // 2
    width = tokens.shape[1]
    context_place = lax.axis_index("context")
    core = lax.axis_index("tensor") % 2
    pair = lax.axis_index("tensor") // 2
    reach = min(lax.axis_size("context") - 1, (LMAX - 2) // block_rows + 1)
    dp_count = lax.axis_size("dp")
    shard = width // dp_count
    feed_width = gate_weight.shape[1]

    lanes = 2 * HD
    head_shard = HD // dp_count
    gains = jnp.concatenate(
        [
            stacked_rows([input_gain, attention_gain, prefeed_gain, feed_gain], 16),
            stacked_rows([query_gain, key_gain], 16),
        ],
        axis=1,
    )
    w_key = dp_gathered(key_weight)
    w_value = dp_gathered(value_weight)
    gain_parts = dp_gathered(gains).reshape(dp_count, 16, shard + head_shard)
    query_weight, output_weight = after((query_weight, output_weight), (w_key, w_value))
    w_query = dp_gathered(query_weight)
    w_out = dp_gathered(output_weight, axis=1)
    gate_weight, up_weight, down_weight = after(
        (gate_weight, up_weight, down_weight.T), (w_query, w_out)
    )
    w_gate, w_up, w_down = (dp_gathered(w) for w in (gate_weight, up_weight, down_weight))

    def gain_of(number, first, count):
        return gain_parts[:, number, first : first + count].reshape(1, -1).astype(F32)

    g_input, g_attention, g_prefeed, g_feed = (gain_of(i, 0, shard) for i in range(4))
    g_query, g_key = (gain_of(i, shard, head_shard) for i in (0, 1))

    stream = lax.dynamic_slice_in_dim(tokens, core * rows, rows, 0).astype(F32)
    grad_out = lax.dynamic_slice_in_dim(cotangent, core * rows, rows, 0).astype(F32)
    row_index = (
        context_place * block_rows + core * rows + lax.broadcasted_iota(jnp.int32, (rows, 1), 0)
    )
    start = jnp.zeros_like(row_index)
    begin = jnp.int32(0)
    for number in range(seq_lengths.shape[1]):
        start = jnp.where(row_index >= begin, begin, start)
        begin = begin + seq_lengths[0, number]
    frequency = jnp.exp(
        lax.broadcasted_iota(jnp.int32, (1, HD // 2), 1).astype(F32)
        * (-2.0 * math.log(1000000.0) / HD)
    )
    angles = (row_index - start).astype(F32) * frequency
    cosines, sines = lax.optimization_barrier((jnp.cos(angles), jnp.sin(angles)))
    two_cosines = jnp.concatenate([cosines, cosines], axis=0)
    two_sines = jnp.concatenate([sines, sines], axis=0)

    input_unit, input_inverse = normed_of(stream)
    normed = (input_unit * g_input).astype(BF)

    w_kv = jnp.concatenate([w_key, w_value], axis=1)
    key_value_raw = product(normed, w_kv)
    key_unit, key_inverse = normed_of(key_value_raw[:, :HD])
    kv_own = jnp.concatenate(
        [
            turned(key_unit * g_key, cosines, sines).astype(BF),
            key_value_raw[:, HD:].astype(BF),
        ],
        axis=1,
    )
    piece = rows // 2

    def piece_of(array, own=True):
        return lax.dynamic_slice_in_dim(array, (pair if own else 1 - pair) * piece, piece, 0)

    current = (kv_own[:, :HD], kv_own[:, HD:])
    arrived = [kv_own]
    for step in range(reach):
        current = (over_context(current[0], 1), over_context(current[1], 1))
        arrived.append(jnp.concatenate(current, axis=1))

    w_query, w_out = after((w_query, w_out), arrived[max(reach - 1, 0)])
    w_query_two = jnp.concatenate([w_query, over_core(w_query)], axis=1)
    w_output = jnp.concatenate([w_out, over_core(w_out)], axis=0)
    g_attention, g_prefeed, g_feed = after((g_attention, g_prefeed, g_feed), arrived[1])
    query_raw = product(normed, w_query_two)
    query_raw = jnp.concatenate([query_raw[:, :HD], query_raw[:, HD:]], axis=0)
    query_unit, query_inverse = normed_of(query_raw)
    query = turned(query_unit * g_query, two_cosines, two_sines).astype(BF)

    two_rows = jnp.concatenate([row_index, row_index], axis=0)
    two_starts = jnp.concatenate([start, start], axis=0)
    within = lax.broadcasted_iota(jnp.int32, (1, rows), 1)
    key_rows = jnp.concatenate([core * rows + within, (1 - core) * rows + within], axis=1)
    blocks = []
    kept = []
    mass = jnp.zeros((2 * rows, 1), F32)
    heads_sum = jnp.zeros((2 * rows, HD), F32)
    for step in range(reach + 1):
        both = arrived[step]
        if step == reach:
            both = after(both, (mass, heads_sum, w_output, g_attention, g_prefeed, g_feed))
        both = jnp.concatenate([both, over_core(both)], axis=0)
        key_block, value_block = both[:, :HD], both[:, HD:]
        blocks.append((key_block, value_block))
        key_index = (context_place - step) * block_rows + key_rows
        allowed = (key_index >= two_starts) & (key_index <= two_rows)
        weights = jnp.where(allowed, jnp.exp(product_rt(query, key_block) * SCALE), 0.0)
        mass = mass + jnp.sum(weights, axis=1, keepdims=True)
        weights = weights.astype(BF)
        heads_sum = heads_sum + product(weights, value_block)
        kept.append(weights)
    inverse_mass = 1.0 / mass
    heads = heads_sum * inverse_mass
    heads_low = heads.astype(BF)
    heads_wide = jnp.concatenate([heads_low[:rows], heads_low[rows:]], axis=1)
    attn_part = low(product(heads_wide, w_output))
    attn_other = over_pairs(attn_part)
    w_gate, w_up, w_down = after((w_gate, w_up, w_down), attn_part)
    w_gate_up = jnp.concatenate([w_gate, over_core(w_gate), w_up, over_core(w_up)], axis=1)
    w_down = jnp.concatenate([w_down, over_core(w_down)], axis=1)
    attn_other = after(attn_other, (w_gate_up, w_down))
    attn_sum = attn_part.astype(F32) + attn_other.astype(F32)

    attn_unit, attn_inverse = normed_of(attn_sum)
    middle = stream + attn_unit * g_attention
    middle_unit, middle_inverse = normed_of(middle)
    normed_feed = (middle_unit * g_prefeed).astype(BF)
    gate_up = product(normed_feed, w_gate_up)
    activation, activation_back = jax.vjp(
        lambda gate_part, up_part: jax.nn.gelu(gate_part, approximate=True) * up_part,
        gate_up[:, : 2 * feed_width],
        gate_up[:, 2 * feed_width :],
    )
    hidden = activation.astype(BF)
    feed_sum = pairs_sum(product_rt(hidden, w_down))
    feed_unit, feed_inverse = normed_of(feed_sum)
    layer_own = low(middle + feed_unit * g_feed)
    layer_out = ordered(core, layer_own, over_core(layer_own))

    grad_gfeed = jnp.sum(grad_out * feed_unit, axis=0, keepdims=True)
    grad_feed = norm_back(grad_out, g_feed, feed_unit, feed_inverse).astype(BF)
    grad_gate_full, grad_up_full = activation_back(product(grad_feed, w_down))
    grad_gate_up = jnp.concatenate([grad_gate_full.astype(BF), grad_up_full.astype(BF)], axis=1)
    def shared(total, own, other):
        mine = jnp.concatenate([total[:, a:b] for a, b in own], axis=1)
        theirs = jnp.concatenate([total[:, a:b] for a, b in other], axis=1)
        return mine, low(theirs)

    parts_down = shared(
        product_lt(grad_feed, hidden), [(0, feed_width)], [(feed_width, 2 * feed_width)]
    )
    whole_down = parts_down[0] + over_core(parts_down[1]).astype(F32)
    feed_part = low(product_rt(grad_gate_up, w_gate_up))
    feed_other = over_pairs(feed_part)
    parts_gate_up = shared(
        product_lt(*after((normed_feed, grad_gate_up), feed_part)),
        [(0, feed_width), (2 * feed_width, 3 * feed_width)],
        [(feed_width, 2 * feed_width), (3 * feed_width, 4 * feed_width)],
    )
    whole_gate_up = parts_gate_up[0] + over_core(parts_gate_up[1]).astype(F32)
    shard_down = dp_scattered(whole_down)
    feed_other = after(feed_other, (whole_gate_up, shard_down, layer_out))
    grad_normed_feed = feed_part.astype(F32) + feed_other.astype(F32)
    shard_gate_up = dp_scattered(whole_gate_up)
    near_down = sum_near(shard_down)

    grad_gprefeed = jnp.sum(grad_normed_feed * middle_unit, axis=0, keepdims=True)
    grad_middle = grad_out + norm_back(grad_normed_feed, g_prefeed, middle_unit, middle_inverse)
    grad_gattention = jnp.sum(grad_middle * attn_unit, axis=0, keepdims=True)
    grad_attn = norm_back(grad_middle, g_attention, attn_unit, attn_inverse).astype(BF)

    grad_heads_wide = product_rt(grad_attn, w_output)
    grad_heads = jnp.concatenate([grad_heads_wide[:, :HD], grad_heads_wide[:, HD:]], axis=0)
    grad_heads_low = (grad_heads * inverse_mass).astype(BF)
    row_dots = jnp.sum(grad_heads * heads, axis=1, keepdims=True) * inverse_mass
    grad_query = jnp.zeros((2 * rows, HD), F32)
    block_grads = {}
    for step in range(reach, -1, -1):
        key_block, value_block = blocks[step]
        weights = kept[step]
        if step == reach - 1:
            weights = after(weights, (near_down, block_grads[reach]))
            far_down = sum_far(near_down)
        if step == reach - 2:
            weights = after(weights, (far_down, block_grads[reach - 1]))
            all_down = spread_far(far_down)
        if step == 0:
            weights = after(weights, (shard_gate_up, all_down, block_grads[1]))
            near_gate_up = sum_near(shard_gate_up)
        grad_scores = (
            weights.astype(F32) * (product_rt(grad_heads_low, value_block) - row_dots)
        ).astype(BF)
        block_grads[step] = jnp.concatenate(
            [product_lt(grad_scores, query) * SCALE, product_lt(weights, grad_heads_low)], axis=1
        )
        grad_query = grad_query + product(grad_scores, key_block)
    grad_query_turned = turned(grad_query * SCALE, two_cosines, -two_sines)
    grad_gquery = jnp.sum(grad_query_turned * query_unit, axis=0, keepdims=True)
    grad_query_raw = norm_back(grad_query_turned, g_query, query_unit, query_inverse).astype(BF)
    grad_query_wide = jnp.concatenate([grad_query_raw[:rows], grad_query_raw[rows:]], axis=1)
    grad_normed_query = product_rt(grad_query_wide, w_query_two)
    parts_qo = shared(
        jnp.concatenate(
            [product_lt(normed, grad_query_wide), product_lt(grad_attn, heads_wide)], axis=1
        ),
        [(0, HD), (2 * HD, 3 * HD)],
        [(HD, 2 * HD), (3 * HD, 4 * HD)],
    )
    whole_qo = parts_qo[0] + over_core(parts_qo[1]).astype(F32)

    def group_sum(group, first_due, then_due):
        theirs = over_core(jnp.concatenate([low(block_grads[s][rows:]) for s in group], axis=0))
        if first_due is not None:
            theirs = after(theirs, first_due)
        mine = jnp.concatenate([block_grads[s][:rows] for s in group], axis=0) + theirs.astype(F32)
        mine = mine.reshape(len(group), rows, lanes)
        keep = lax.dynamic_slice_in_dim(mine, pair * piece, piece, 1)
        send = low(lax.dynamic_slice_in_dim(mine, (1 - pair) * piece, piece, 1))
        other = over_pairs(send)
        if then_due is not None:
            other = after(other, then_due)
        return keep + other.astype(F32)

    far_group = list(range(reach, 1, -1))
    near_group = [1, 0]
    far_sums = group_sum(far_group, near_gate_up, whole_qo)
    far_gate_up = sum_far(near_gate_up)
    shard_qo = dp_scattered(whole_qo)
    far_parts = [
        over_context(low(far_sums[number]), -step) for number, step in enumerate(far_group)
    ]
    near_sums = group_sum(near_group, far_gate_up, far_parts[0])
    near_part = over_context(low(near_sums[0]), -1)
    all_gate_up = spread_far(far_gate_up)
    grad_normed_query_low = low(after(grad_normed_query, near_sums))
    far_parts, near_part = after((far_parts, near_part), (shard_qo, all_gate_up))
    grad_kv = near_sums[1] + near_part.astype(F32)
    for part in far_parts:
        grad_kv = grad_kv + part.astype(F32)
    grad_normed = grad_normed_query_low.astype(F32) + over_pairs(grad_normed_query_low).astype(F32)

    piece_unit = piece_of(key_unit)
    grad_key_turned = turned(grad_kv[:, :HD], piece_of(cosines), -piece_of(sines))
    grad_gkey = jnp.sum(grad_key_turned * piece_unit, axis=0, keepdims=True)
    grad_key_raw = norm_back(grad_key_turned, g_key, piece_unit, piece_of(key_inverse)).astype(BF)
    grad_kv_raw = jnp.concatenate([grad_key_raw, grad_kv[:, HD:].astype(BF)], axis=1)
    grad_normed_kv = low(product_rt(grad_kv_raw, w_kv))
    grad_ginput = jnp.sum(grad_normed_query * input_unit, axis=0, keepdims=True) + jnp.sum(
        grad_normed_kv.astype(F32) * piece_of(input_unit), axis=0, keepdims=True
    )

    once = jnp.where(pair == 0, 1.0, 0.0).astype(F32)
    long_grads = [
        grad_ginput, grad_gattention * once, grad_gprefeed * once, grad_gfeed * once
    ]
    gain_rows = [
        jnp.pad(
            jnp.concatenate(
                [
                    stacked_rows([g[:, i * shard : (i + 1) * shard] for g in long_grads], 16),
                    stacked_rows(
                        [
                            g[:, i * head_shard : (i + 1) * head_shard]
                            for g in (grad_gquery, grad_gkey)
                        ],
                        16,
                    ),
                ],
                axis=1,
            ),
            ((0, 0), (0, lanes - shard - head_shard)),
        )
        for i in range(dp_count)
    ]
    grad_w_kv = product_lt(piece_of(normed), grad_kv_raw)
    small = jnp.concatenate(
        [
            part
            for i in range(dp_count)
            for part in (
                grad_w_kv[i * shard : (i + 1) * shard],
                gain_rows[i],
            )
        ],
        axis=0,
    )
    columns = lanes // 2
    send = low(lax.dynamic_slice_in_dim(small, (1 - core) * columns, columns, 1))
    other = over_core(send)
    near_qo = sum_near(after(shard_qo, send))
    grad_normed_kv = after(grad_normed_kv, send)
    small = lax.dynamic_slice_in_dim(small, core * columns, columns, 1) + other.astype(F32)
    far_qo = sum_far(after(near_qo, small))
    small = owners_sum(small, columns // 2)
    other = over_pairs(grad_normed_kv)
    grad_normed = grad_normed + ordered(pair, grad_normed_kv, other).astype(F32)
    tokens_own = grad_middle + norm_back(grad_normed, g_input, input_unit, input_inverse)
    tokens_other = over_core(tokens_own)
    small = after(small, far_qo)
    total_gate_up = spread_near(all_gate_up)
    all_qo = spread_far(far_qo)
    small = low(context_sum_small(small))
    total_qo = spread_near(all_qo)
    total_down = spread_near(all_down)
    tokens_grad = ordered(core, tokens_own, tokens_other)
    over_both = partner(small, 0, 3)
    other_core = over_core(small)
    small = ordered(pair, small, over_pairs(small), axis=1)
    small = ordered(core, small, ordered(pair, other_core, over_both, axis=1), axis=1).astype(F32)

    return (
        layer_out,
        tokens_grad,
        small[shard, :shard],
        total_qo[:, :HD],
        small[:shard, :HD],
        small[:shard, HD:],
        small[shard, shard : shard + head_shard],
        small[shard + 1, shard : shard + head_shard],
        total_qo[:, HD:].T,
        small[shard + 1, :shard],
        small[shard + 2, :shard],
        total_gate_up[:, :feed_width],
        total_gate_up[:, feed_width:],
        total_down.T,
        small[shard + 3, :shard],
    )


def solution(mesh):
    placed = (
        P(("dp", "context"), None),
        P("dp", None),
        P("dp"),
        P("dp", "tensor"),
        P("dp", None),
        P("dp", None),
        P("dp"),
        P("dp"),
        P("tensor", "dp"),
        P("dp"),
        P("dp"),
        P("dp", "tensor"),
        P("dp", "tensor"),
        P("tensor", "dp"),
        P("dp"),
        P(("dp", "context"), None),
    )
    return jax.shard_map(
        local,
        mesh=mesh,
        in_specs=placed,
        out_specs=(
            P(("dp", "context"), None),
            P(("dp", "context"), None),
            P("dp"),
            P("dp", "tensor"),
            P("dp", None),
            P("dp", None),
            P("dp"),
            P("dp"),
            P("tensor", "dp"),
            P("dp"),
            P("dp"),
            P("dp", "tensor"),
            P("dp", "tensor"),
            P("tensor", "dp"),
            P("dp"),
        ),
        check_vma=False,
    )
```

```python
import math

import jax
import jax.numpy as jnp
from jax import lax
from jax.sharding import PartitionSpec as P

HD = 256
LMAX = 2048
EPS = 1e-06
SCALE = 0.0625

BF = jnp.bfloat16
F32 = jnp.float32


def product(left_side, right_side):
    return jnp.dot(left_side, right_side, preferred_element_type=F32)


def product_lt(left_side, right_side):
    return lax.dot_general(
        left_side, right_side, (((0,), (0,)), ((), ())), preferred_element_type=F32
    )


def product_rt(left_side, right_side):
    return lax.dot_general(
        left_side, right_side, (((1,), (1,)), ((), ())), preferred_element_type=F32
    )


def low(values):
    return lax.reduce_precision(values, 8, 7).astype(BF)


def over_core(array):
    devices = lax.axis_size("tensor")
    return lax.ppermute(array, "tensor", [(i, i ^ 1) for i in range(devices)])


def over_pairs(array):
    devices = lax.axis_size("tensor")
    return lax.ppermute(array, "tensor", [(i, i ^ 2) for i in range(devices)])


def over_context(array, by):
    devices = lax.axis_size("context")
    pairs = [(i, i + by) for i in range(devices) if 0 <= i + by < devices]
    return lax.ppermute(array, "context", pairs)


def after(array, earlier):
    return lax.optimization_barrier((array, earlier))[0]


def ordered(place, mine, other, axis=0):
    first = place == 0
    return jnp.concatenate(
        [jnp.where(first, mine, other), jnp.where(first, other, mine)], axis=axis
    )


def pairs_sum(partial, meanwhile=None):
    short = low(partial)
    other = over_pairs(short)
    if meanwhile is not None:
        other = after(other, meanwhile)
    return short.astype(F32) + other.astype(F32)


def stacked_rows(vectors, rows):
    lanes = vectors[0].size
    place = lax.broadcasted_iota(jnp.int32, (rows, lanes), 0)
    total = jnp.zeros((rows, lanes), vectors[0].dtype)
    for number, vector in enumerate(vectors):
        wide = lax.broadcast_in_dim(vector.reshape(-1), (rows, lanes), (1,))
        total = jnp.where(place == number, wide, total)
    return total


def dp_gathered(array, axis=0):
    if lax.axis_size("dp") == 2:
        other = lax.ppermute(array, "dp", [(0, 1), (1, 0)])
        return ordered(lax.axis_index("dp"), array, other, axis)
    return lax.all_gather(array, "dp", axis=axis, tiled=True)


def dp_scattered(total):
    if lax.axis_size("dp") == 2:
        place = lax.axis_index("dp")
        rows = total.shape[0] // 2
        keep = lax.dynamic_slice_in_dim(total, place * rows, rows, 0)
        send = lax.dynamic_slice_in_dim(total, (1 - place) * rows, rows, 0)
        return keep.astype(F32) + lax.ppermute(low(send), "dp", [(0, 1), (1, 0)]).astype(F32)
    return lax.psum_scatter(low(total), "dp", scatter_dimension=0, tiled=True).astype(F32)


def sum_near(total):
    if lax.axis_size("context") != 4:
        return lax.psum(low(total), "context")
    near = lax.axis_index("context") % 2
    rows = total.shape[0] // 2
    keep = lax.dynamic_slice_in_dim(total, near * rows, rows, 0)
    send = lax.dynamic_slice_in_dim(total, (1 - near) * rows, rows, 0)
    return keep + lax.ppermute(low(send), "context", [(i, i ^ 1) for i in range(4)]).astype(F32)


def sum_far(part):
    if lax.axis_size("context") != 4:
        return part
    far = lax.axis_index("context") // 2
    rows = part.shape[0] // 2
    keep = lax.dynamic_slice_in_dim(part, far * rows, rows, 0)
    send = lax.dynamic_slice_in_dim(part, (1 - far) * rows, rows, 0)
    return low(keep + lax.ppermute(low(send), "context", [(i, i ^ 2) for i in range(4)]).astype(F32))


def spread_far(part):
    if lax.axis_size("context") != 4:
        return part
    other = lax.ppermute(part, "context", [(i, i ^ 2) for i in range(4)])
    return ordered(lax.axis_index("context") // 2, part, other)


def spread_near(part):
    if lax.axis_size("context") != 4:
        return part.astype(F32)
    other = lax.ppermute(part, "context", [(i, i ^ 1) for i in range(4)])
    return ordered(lax.axis_index("context") % 2, part, other).astype(F32)


def context_sum_small(total):
    if lax.axis_size("context") != 4:
        return lax.psum(total, "context")
    short = low(total)
    other = [
        lax.ppermute(short, "context", [(i, (i + by) % 4) for i in range(4)]).astype(F32)
        for by in (1, 2, 3)
    ]
    return (short.astype(F32) + other[1]) + (other[0] + other[2])


def partner(array, dp_turn, tensor_turn):
    count = lax.axis_size("tensor")
    pairs = [
        (i * count + j, (i ^ dp_turn) * count + (j ^ tensor_turn))
        for i in range(lax.axis_size("dp"))
        for j in range(count)
    ]
    return lax.ppermute(array, ("dp", "tensor"), pairs)


def owners_sum(total, columns):
    place = lax.axis_index("dp")
    pair = lax.axis_index("tensor") // 2
    rows = total.shape[0] // lax.axis_size("dp")
    if lax.axis_size("dp") != 2:
        total = lax.dynamic_slice_in_dim(total, pair * columns, columns, 1) + over_pairs(
            low(lax.dynamic_slice_in_dim(total, (1 - pair) * columns, columns, 1))
        ).astype(F32)
        return dp_scattered(total)

    def part(dp_turn, pair_turn):
        at = (jnp.bitwise_xor(place, dp_turn) * rows, jnp.bitwise_xor(pair, pair_turn) * columns)
        return lax.dynamic_slice(total, at, (rows, columns))

    whole = part(0, 0)
    for dp_turn, pair_turn in ((0, 1), (1, 0), (1, 1)):
        short = low(part(dp_turn, pair_turn))
        whole = whole + partner(short, dp_turn, 2 * pair_turn).astype(F32)
    return whole


def normed_of(values):
    inverse = lax.rsqrt(jnp.mean(values * values, axis=-1, keepdims=True) + EPS)
    return values * inverse, inverse


def norm_back(grad, gain, unit, inverse):
    scaled = grad * gain
    return inverse * (scaled - unit * jnp.mean(scaled * unit, axis=-1, keepdims=True))


def turned(values, cosines, sines):
    half_width = values.shape[-1] // 2
    first_half = values[..., :half_width]
    second_half = values[..., half_width:]
    return jnp.concatenate(
        [first_half * cosines - second_half * sines, second_half * cosines + first_half * sines],
        axis=-1,
    )


def local(
    tokens,
    seq_lengths,
    input_gain,
    query_weight,
    key_weight,
    value_weight,
    query_gain,
    key_gain,
    output_weight,
    attention_gain,
    prefeed_gain,
    gate_weight,
    up_weight,
    down_weight,
    feed_gain,
    cotangent,
):
    block_rows = tokens.shape[0]
    rows = block_rows // 2
    width = tokens.shape[1]
    context_place = lax.axis_index("context")
    core = lax.axis_index("tensor") % 2
    pair = lax.axis_index("tensor") // 2
    reach = min(lax.axis_size("context") - 1, (LMAX - 2) // block_rows + 1)
    dp_count = lax.axis_size("dp")
    shard = width // dp_count
    feed_width = gate_weight.shape[1]

    lanes = 2 * HD
    head_shard = HD // dp_count
    gains = jnp.concatenate(
        [
            stacked_rows([input_gain, attention_gain, prefeed_gain, feed_gain], 16),
            stacked_rows([query_gain, key_gain], 16),
        ],
        axis=1,
    )
    w_key = dp_gathered(key_weight)
    w_value = dp_gathered(value_weight)
    gain_parts = dp_gathered(gains).reshape(dp_count, 16, shard + head_shard)
    w_key, w_value, query_weight, output_weight = lax.optimization_barrier(
        (w_key, w_value, query_weight, output_weight)
    )
    w_query = dp_gathered(query_weight)
    w_out = dp_gathered(output_weight, axis=1)
    gate_weight, up_weight, down_weight = after(
        (gate_weight, up_weight, down_weight.T), (w_query, w_out)
    )
    w_gate, w_up, w_down = (dp_gathered(w) for w in (gate_weight, up_weight, down_weight))

    def gain_of(number, first, count):
        return gain_parts[:, number, first : first + count].reshape(1, -1).astype(F32)

    g_input, g_attention, g_prefeed, g_feed = (gain_of(i, 0, shard) for i in range(4))
    g_query, g_key = (gain_of(i, shard, head_shard) for i in (0, 1))

    stream = lax.dynamic_slice_in_dim(tokens, core * rows, rows, 0).astype(F32)
    grad_out = lax.dynamic_slice_in_dim(cotangent, core * rows, rows, 0).astype(F32)
    row_index = (
        context_place * block_rows + core * rows + lax.broadcasted_iota(jnp.int32, (rows, 1), 0)
    )
    start = jnp.zeros_like(row_index)
    begin = jnp.int32(0)
    for number in range(seq_lengths.shape[1]):
        start = jnp.where(row_index >= begin, begin, start)
        begin = begin + seq_lengths[0, number]
    frequency = jnp.exp(
        lax.broadcasted_iota(jnp.int32, (1, HD // 2), 1).astype(F32)
        * (-2.0 * math.log(1000000.0) / HD)
    )
    angles = (row_index - start).astype(F32) * frequency
    cosines, sines = lax.optimization_barrier((jnp.cos(angles), jnp.sin(angles)))
    two_cosines = jnp.concatenate([cosines, cosines], axis=0)
    two_sines = jnp.concatenate([sines, sines], axis=0)

    input_unit, input_inverse = normed_of(stream)
    normed = (input_unit * g_input).astype(BF)

    w_kv = jnp.concatenate([w_key, w_value], axis=1)
    key_value_raw = product(normed, w_kv)
    key_unit, key_inverse = normed_of(key_value_raw[:, :HD])
    kv_own = jnp.concatenate(
        [
            turned(key_unit * g_key, cosines, sines).astype(BF),
            key_value_raw[:, HD:].astype(BF),
        ],
        axis=1,
    )
    piece = rows // 2

    def piece_of(array, own=True):
        return lax.dynamic_slice_in_dim(array, (pair if own else 1 - pair) * piece, piece, 0)

    current = (kv_own[:, :HD], kv_own[:, HD:])
    arrived = [kv_own]
    for step in range(reach):
        current = (over_context(current[0], 1), over_context(current[1], 1))
        arrived.append(jnp.concatenate(current, axis=1))

    w_query, w_out = after((w_query, w_out), arrived[max(reach - 1, 0)])
    w_query_two = jnp.concatenate([w_query, over_core(w_query)], axis=1)
    w_output = jnp.concatenate([w_out, over_core(w_out)], axis=0)
    g_attention, g_prefeed, g_feed = after((g_attention, g_prefeed, g_feed), arrived[1])
    query_raw = product(normed, w_query_two)
    query_raw = jnp.concatenate([query_raw[:, :HD], query_raw[:, HD:]], axis=0)
    query_unit, query_inverse = normed_of(query_raw)
    query = turned(query_unit * g_query, two_cosines, two_sines).astype(BF)

    two_rows = jnp.concatenate([row_index, row_index], axis=0)
    two_starts = jnp.concatenate([start, start], axis=0)
    within = lax.broadcasted_iota(jnp.int32, (1, rows), 1)
    key_rows = jnp.concatenate([core * rows + within, (1 - core) * rows + within], axis=1)
    blocks = []
    kept = []
    mass = jnp.zeros((2 * rows, 1), F32)
    heads_sum = jnp.zeros((2 * rows, HD), F32)
    for step in range(reach + 1):
        both = arrived[step]
        if step == reach:
            both = after(both, (mass, heads_sum, w_output, g_attention, g_prefeed, g_feed))
        both = jnp.concatenate([both, over_core(both)], axis=0)
        key_block, value_block = both[:, :HD], both[:, HD:]
        blocks.append((key_block, value_block))
        key_index = (context_place - step) * block_rows + key_rows
        allowed = (key_index >= two_starts) & (key_index <= two_rows)
        weights = jnp.where(allowed, jnp.exp(product_rt(query, key_block) * SCALE), 0.0)
        mass = mass + jnp.sum(weights, axis=1, keepdims=True)
        weights = weights.astype(BF)
        heads_sum = heads_sum + product(weights, value_block)
        kept.append(weights)
    inverse_mass = 1.0 / mass
    heads = heads_sum * inverse_mass
    heads_low = heads.astype(BF)
    heads_wide = jnp.concatenate([heads_low[:rows], heads_low[rows:]], axis=1)
    attn_part = low(product(heads_wide, w_output))
    attn_other = over_pairs(attn_part)
    w_gate, w_up, w_down = after((w_gate, w_up, w_down), attn_part)
    w_gate_up = jnp.concatenate([w_gate, over_core(w_gate), w_up, over_core(w_up)], axis=1)
    w_down = jnp.concatenate([w_down, over_core(w_down)], axis=1)
    attn_other = after(attn_other, (w_gate_up, w_down))
    attn_sum = attn_part.astype(F32) + attn_other.astype(F32)

    attn_unit, attn_inverse = normed_of(attn_sum)
    middle = stream + attn_unit * g_attention
    middle_unit, middle_inverse = normed_of(middle)
    normed_feed = (middle_unit * g_prefeed).astype(BF)
    gate_up = product(normed_feed, w_gate_up)
    activation, activation_back = jax.vjp(
        lambda gate_part, up_part: jax.nn.gelu(gate_part, approximate=True) * up_part,
        gate_up[:, : 2 * feed_width],
        gate_up[:, 2 * feed_width :],
    )
    hidden = activation.astype(BF)
    feed_sum = pairs_sum(product_rt(hidden, w_down))
    feed_unit, feed_inverse = normed_of(feed_sum)
    layer_own = low(middle + feed_unit * g_feed)
    layer_out = ordered(core, layer_own, over_core(layer_own))

    grad_gfeed = jnp.sum(grad_out * feed_unit, axis=0, keepdims=True)
    grad_feed = norm_back(grad_out, g_feed, feed_unit, feed_inverse).astype(BF)
    grad_gate_full, grad_up_full = activation_back(product(grad_feed, w_down))
    grad_gate_up = jnp.concatenate([grad_gate_full.astype(BF), grad_up_full.astype(BF)], axis=1)
    def shared(total, own, other):
        mine = jnp.concatenate([total[:, a:b] for a, b in own], axis=1)
        theirs = jnp.concatenate([total[:, a:b] for a, b in other], axis=1)
        return mine, low(theirs)

    parts_down = shared(
        product_lt(grad_feed, hidden), [(0, feed_width)], [(feed_width, 2 * feed_width)]
    )
    whole_down = parts_down[0] + over_core(parts_down[1]).astype(F32)
    feed_part = low(product_rt(grad_gate_up, w_gate_up))
    feed_other = over_pairs(feed_part)
    parts_gate_up = shared(
        product_lt(*after((normed_feed, grad_gate_up), feed_part)),
        [(0, feed_width), (2 * feed_width, 3 * feed_width)],
        [(feed_width, 2 * feed_width), (3 * feed_width, 4 * feed_width)],
    )
    whole_gate_up = parts_gate_up[0] + over_core(parts_gate_up[1]).astype(F32)
    shard_down = dp_scattered(whole_down)
    feed_other = after(feed_other, (whole_gate_up, shard_down, layer_out))
    grad_normed_feed = feed_part.astype(F32) + feed_other.astype(F32)
    shard_gate_up = dp_scattered(whole_gate_up)
    near_down = sum_near(shard_down)

    grad_gprefeed = jnp.sum(grad_normed_feed * middle_unit, axis=0, keepdims=True)
    grad_middle = grad_out + norm_back(grad_normed_feed, g_prefeed, middle_unit, middle_inverse)
    grad_gattention = jnp.sum(grad_middle * attn_unit, axis=0, keepdims=True)
    grad_attn = norm_back(grad_middle, g_attention, attn_unit, attn_inverse).astype(BF)

    grad_heads_wide = product_rt(grad_attn, w_output)
    grad_heads = jnp.concatenate([grad_heads_wide[:, :HD], grad_heads_wide[:, HD:]], axis=0)
    grad_heads_low = (grad_heads * inverse_mass).astype(BF)
    row_dots = jnp.sum(grad_heads * heads, axis=1, keepdims=True) * inverse_mass
    grad_query = jnp.zeros((2 * rows, HD), F32)
    block_grads = {}
    for step in range(reach, -1, -1):
        key_block, value_block = blocks[step]
        weights = kept[step]
        if step == reach - 1:
            weights = after(weights, (near_down, block_grads[reach]))
            far_down = sum_far(near_down)
        if step == reach - 2:
            weights = after(weights, (far_down, block_grads[reach - 1]))
            all_down = spread_far(far_down)
        if step == 0:
            weights = after(weights, (shard_gate_up, all_down, block_grads[1]))
            near_gate_up = sum_near(shard_gate_up)
        grad_scores = (
            weights.astype(F32) * (product_rt(grad_heads_low, value_block) - row_dots)
        ).astype(BF)
        block_grads[step] = jnp.concatenate(
            [product_lt(grad_scores, query) * SCALE, product_lt(weights, grad_heads_low)], axis=1
        )
        grad_query = grad_query + product(grad_scores, key_block)
    grad_query_turned = turned(grad_query * SCALE, two_cosines, -two_sines)
    grad_gquery = jnp.sum(grad_query_turned * query_unit, axis=0, keepdims=True)
    grad_query_raw = norm_back(grad_query_turned, g_query, query_unit, query_inverse).astype(BF)
    grad_query_wide = jnp.concatenate([grad_query_raw[:rows], grad_query_raw[rows:]], axis=1)
    grad_normed_query = product_rt(grad_query_wide, w_query_two)
    parts_qo = shared(
        jnp.concatenate(
            [product_lt(normed, grad_query_wide), product_lt(grad_attn, heads_wide)], axis=1
        ),
        [(0, HD), (2 * HD, 3 * HD)],
        [(HD, 2 * HD), (3 * HD, 4 * HD)],
    )
    whole_qo = parts_qo[0] + over_core(parts_qo[1]).astype(F32)

    def group_sum(group, first_due, then_due):
        theirs = over_core(jnp.concatenate([low(block_grads[s][rows:]) for s in group], axis=0))
        if first_due is not None:
            theirs = after(theirs, first_due)
        mine = jnp.concatenate([block_grads[s][:rows] for s in group], axis=0) + theirs.astype(F32)
        mine = mine.reshape(len(group), rows, lanes)
        keep = lax.dynamic_slice_in_dim(mine, pair * piece, piece, 1)
        send = low(lax.dynamic_slice_in_dim(mine, (1 - pair) * piece, piece, 1))
        other = over_pairs(send)
        if then_due is not None:
            other = after(other, then_due)
        return keep + other.astype(F32)

    far_group = list(range(reach, 1, -1))
    near_group = [1, 0]
    far_sums = group_sum(far_group, near_gate_up, whole_qo)
    far_gate_up = sum_far(near_gate_up)
    shard_qo = dp_scattered(whole_qo)
    far_parts = [
        over_context(low(far_sums[number]), -step) for number, step in enumerate(far_group)
    ]
    near_sums = group_sum(near_group, far_gate_up, far_parts[0])
    near_part = over_context(low(near_sums[0]), -1)
    all_gate_up = spread_far(far_gate_up)
    grad_normed_query_low = low(after(grad_normed_query, near_sums))
    far_parts, near_part = after((far_parts, near_part), (shard_qo, all_gate_up))
    grad_kv = near_sums[1] + near_part.astype(F32)
    for part in far_parts:
        grad_kv = grad_kv + part.astype(F32)
    grad_normed = grad_normed_query_low.astype(F32) + over_pairs(grad_normed_query_low).astype(F32)

    piece_unit = piece_of(key_unit)
    grad_key_turned = turned(grad_kv[:, :HD], piece_of(cosines), -piece_of(sines))
    grad_gkey = jnp.sum(grad_key_turned * piece_unit, axis=0, keepdims=True)
    grad_key_raw = norm_back(grad_key_turned, g_key, piece_unit, piece_of(key_inverse)).astype(BF)
    grad_kv_raw = jnp.concatenate([grad_key_raw, grad_kv[:, HD:].astype(BF)], axis=1)
    grad_normed_kv = low(product_rt(grad_kv_raw, w_kv))
    grad_ginput = jnp.sum(grad_normed_query * input_unit, axis=0, keepdims=True) + jnp.sum(
        grad_normed_kv.astype(F32) * piece_of(input_unit), axis=0, keepdims=True
    )

    once = jnp.where(pair == 0, 1.0, 0.0).astype(F32)
    long_grads = [
        grad_ginput, grad_gattention * once, grad_gprefeed * once, grad_gfeed * once
    ]
    gain_rows = [
        jnp.pad(
            jnp.concatenate(
                [
                    stacked_rows([g[:, i * shard : (i + 1) * shard] for g in long_grads], 16),
                    stacked_rows(
                        [
                            g[:, i * head_shard : (i + 1) * head_shard]
                            for g in (grad_gquery, grad_gkey)
                        ],
                        16,
                    ),
                ],
                axis=1,
            ),
            ((0, 0), (0, lanes - shard - head_shard)),
        )
        for i in range(dp_count)
    ]
    grad_w_kv = product_lt(piece_of(normed), grad_kv_raw)
    small = jnp.concatenate(
        [
            part
            for i in range(dp_count)
            for part in (
                grad_w_kv[i * shard : (i + 1) * shard],
                gain_rows[i],
            )
        ],
        axis=0,
    )
    columns = lanes // 2
    send = low(lax.dynamic_slice_in_dim(small, (1 - core) * columns, columns, 1))
    other = over_core(send)
    near_qo = sum_near(after(shard_qo, send))
    grad_normed_kv = after(grad_normed_kv, send)
    small = lax.dynamic_slice_in_dim(small, core * columns, columns, 1) + other.astype(F32)
    far_qo = sum_far(after(near_qo, small))
    small = owners_sum(small, columns // 2)
    other = over_pairs(grad_normed_kv)
    grad_normed = grad_normed + ordered(pair, grad_normed_kv, other).astype(F32)
    tokens_own = low(grad_middle + norm_back(grad_normed, g_input, input_unit, input_inverse))
    tokens_other = over_core(tokens_own)
    small = after(small, far_qo)
    total_gate_up = spread_near(all_gate_up)
    all_qo = spread_far(far_qo)
    small = low(context_sum_small(small))
    total_qo = spread_near(all_qo)
    total_down = spread_near(all_down)
    tokens_grad = ordered(core, tokens_own, tokens_other).astype(F32)
    over_both = partner(small, 0, 3)
    other_core = over_core(small)
    small = ordered(pair, small, over_pairs(small), axis=1)
    small = ordered(core, small, ordered(pair, other_core, over_both, axis=1), axis=1).astype(F32)

    return (
        layer_out,
        tokens_grad,
        small[shard, :shard],
        total_qo[:, :HD],
        small[:shard, :HD],
        small[:shard, HD:],
        small[shard, shard : shard + head_shard],
        small[shard + 1, shard : shard + head_shard],
        total_qo[:, HD:].T,
        small[shard + 1, :shard],
        small[shard + 2, :shard],
        total_gate_up[:, :feed_width],
        total_gate_up[:, feed_width:],
        total_down.T,
        small[shard + 3, :shard],
    )


def solution(mesh):
    placed = (
        P(("dp", "context"), None),
        P("dp", None),
        P("dp"),
        P("dp", "tensor"),
        P("dp", None),
        P("dp", None),
        P("dp"),
        P("dp"),
        P("tensor", "dp"),
        P("dp"),
        P("dp"),
        P("dp", "tensor"),
        P("dp", "tensor"),
        P("tensor", "dp"),
        P("dp"),
        P(("dp", "context"), None),
    )
    return jax.shard_map(
        local,
        mesh=mesh,
        in_specs=placed,
        out_specs=(
            P(("dp", "context"), None),
            P(("dp", "context"), None),
            P("dp"),
            P("dp", "tensor"),
            P("dp", None),
            P("dp", None),
            P("dp"),
            P("dp"),
            P("tensor", "dp"),
            P("dp"),
            P("dp"),
            P("dp", "tensor"),
            P("dp", "tensor"),
            P("tensor", "dp"),
            P("dp"),
        ),
        check_vma=False,
    )
```
